32 devices in a mesh: dp: 8 (over y, x, core), ctx: 4 (over z).
Axes of the slice: x: 2, y: 2, z: 4, core: 2. Of those that a mesh axis runs over, the one named last changes fastest.
Arguments:
- tokens: bfloat16 [16, 2048, 768], P('dp', 'ctx'), may hold values from -6 to 6
- seq_lengths: int32 [16], P('dp'), may hold values from 1025 to 2048, as said below
- attention_gain: bfloat16 [768], P(('dp', 'ctx')), may hold values from 0.5 to 1.5
- attention_bias: bfloat16 [768], P(('dp', 'ctx')), may hold values from -1.5 to 1.5
- query_weight: bfloat16 [768, 768], P(('dp', 'ctx')), may hold values from -0.21875 to 0.21875
- query_bias: bfloat16 [768], P(('dp', 'ctx')), may hold values from -1.5 to 1.5
- keyvalue_weight: bfloat16 [768, 128], P(('dp', 'ctx')), may hold values from -0.21875 to 0.21875
- keyvalue_bias: bfloat16 [128], replicated, may hold values from -1.5 to 1.5
- output_weight: bfloat16 [768, 768], P(('dp', 'ctx')), may hold values from -0.875 to 0.875
- output_bias: bfloat16 [768], P(('dp', 'ctx')), may hold values from -1.5 to 1.5
- feedforward_gain: bfloat16 [768], P(('dp', 'ctx')), may hold values from 0.5 to 1.5
- feedforward_bias: bfloat16 [768], P(('dp', 'ctx')), may hold values from -1.5 to 1.5
- inner_weight: bfloat16 [768, 3072], P(('dp', 'ctx')), may hold values from -0.21875 to 0.21875
- inner_bias: bfloat16 [3072], P(('dp', 'ctx')), may hold values from -1.5 to 1.5
- outer_weight: bfloat16 [3072, 768], P(('dp', 'ctx')), may hold values from -0.109375 to 0.109375
- outer_bias: bfloat16 [768], P(('dp', 'ctx')), may hold values from -1.5 to 1.5
- cotangent: bfloat16 [16, 2048, 768], P('dp', 'ctx'), may hold values from -6 to 6
Outputs:
- outputs: bfloat16 [16, 2048, 768], P('dp', 'ctx')
- token_grads: float32 [16, 2048, 768], P('dp', 'ctx')
- attention_gain_grad: float32 [768], P(('dp', 'ctx'))
- attention_bias_grad: float32 [768], P(('dp', 'ctx'))
- query_weight_grad: float32 [768, 768], P(('dp', 'ctx'))
- query_bias_grad: float32 [768], P(('dp', 'ctx'))
- keyvalue_weight_grad: float32 [768, 128], P(('dp', 'ctx'))
- keyvalue_bias_grad: float32 [128], replicated
- output_weight_grad: float32 [768, 768], P(('dp', 'ctx'))
- output_bias_grad: float32 [768], P(('dp', 'ctx'))
- feedforward_gain_grad: float32 [768], P(('dp', 'ctx'))
- feedforward_bias_grad: float32 [768], P(('dp', 'ctx'))
- inner_weight_grad: float32 [768, 3072], P(('dp', 'ctx'))
- inner_bias_grad: float32 [3072], P(('dp', 'ctx'))
- outer_weight_grad: float32 [3072, 768], P(('dp', 'ctx'))
- outer_bias_grad: float32 [768], P(('dp', 'ctx'))
The draws below stay inside these ranges and needn't reach their ends.
Inputs may be any that keep to these rules, and one draw needn't show every extreme that they name: `seq_lengths`: live tokens at the start of each sequence's 2048 slots; sequence 0 is always full.
All inputs are finite; a program needn't handle non-finite values.
Results may differ from the reference program's by a relative error of at most 0.011.
Values may be sent and summed in bfloat16 or wider, within the bound.
No kernel may reach another device: no remote copies, remote signals or barrier semaphores. Data moves between devices by JAX's collectives and lax.ppermute only.
A program may use at most 192 MiB of HBM per device.

```python
import jax
import jax.numpy as jnp
from jax import lax

D = 768
H = 12
HS = 64
FF = 3072
ROT = 16
LEN = 2048
SEQS = 16


def draw_seq_lengths(key, part):
    values = jax.random.randint(key, (SEQS,), LEN // 2 + 1, LEN + 1)
    return values.at[0].set(LEN).astype(jnp.int32)


def strengthened(values, rng, source, target, blocks, factor):
    def block_of(dim):
        return (jnp.arange(values.shape[dim]) // (values.shape[dim] // blocks)).reshape((-1,) + (1,) * (values.ndim - 1 - dim))

    first = jax.random.permutation(rng, blocks)[block_of(target)]
    far = (block_of(target) + blocks // 2) % blocks
    return jnp.where((block_of(source) == first) | (block_of(source) == far), factor * values, values)


def block_levels(rng, dims, shards, least, largest):
    factor_of, own = 1.0, jax.random.fold_in(rng, 6)
    for dim, blocks in shards:
        steps = jnp.exp(jax.random.uniform(jax.random.fold_in(own, dim), (blocks,), jnp.float32, least / len(shards), largest / len(shards)))
        factor_of = factor_of * jnp.repeat(steps, dims[dim] // blocks).reshape([-1 if axis == dim else 1 for axis in range(len(dims))])
    return factor_of


def bell_draw(stream_key, dims, deviation, most, cuts=(), held_as=jnp.bfloat16):
    drawn = deviation * jax.random.normal(stream_key, dims, jnp.float32)
    if cuts:
        drawn = drawn * block_levels(stream_key, dims, cuts, -0.22, 0.18)
    return jnp.clip(drawn, -most, most).astype(held_as)


def noise_with(stream_key, shape, scale, most, split, heavy, kind=jnp.bfloat16):
    entries = scale * jax.random.normal(stream_key, shape, jnp.float32)
    if split:
        entries = entries * block_levels(stream_key, shape, split, -0.22, 0.18)
    return jnp.clip(strengthened(entries, jax.random.fold_in(stream_key, 3), *heavy), -most, most).astype(kind)


def setup_inputs(seed: int = 0) -> dict:
    streams_of = jax.random.split(jax.random.key(seed), 18)
    return {
        "tokens": noise_with(streams_of[0], (SEQS, LEN, D), 1.0, 6.0, ((0, 8), (1, 4)), (0, 2, 8, 2.0)),
        "seq_lengths": draw_seq_lengths(jax.random.fold_in(streams_of[17], 71), 0),
        "attention_gain": jnp.clip(1.0 + 0.1 * jax.random.normal(streams_of[2], (D,), jnp.float32), 0.5, 1.5).astype(jnp.bfloat16),
        "attention_bias": bell_draw(streams_of[3], (D,), 0.3, 1.5, ((0, 32),)),
        "query_weight": bell_draw(streams_of[4], (D, D), D ** -0.5, 0.21875, ((0, 32),)),
        "query_bias": bell_draw(streams_of[5], (D,), 0.3, 1.5, ((0, 32),)),
        "keyvalue_weight": bell_draw(streams_of[6], (D, 2 * HS), D ** -0.5, 0.21875, ((0, 32),)),
        "keyvalue_bias": bell_draw(streams_of[7], (2 * HS,), 0.3, 1.5),
        "output_weight": bell_draw(streams_of[8], (D, D), (D // 16) ** -0.5, 0.875, ((0, 32),)),
        "output_bias": bell_draw(streams_of[9], (D,), 0.3, 1.5, ((0, 32),)),
        "feedforward_gain": jnp.clip(1.0 + 0.1 * jax.random.normal(streams_of[10], (D,), jnp.float32), 0.5, 1.5).astype(jnp.bfloat16),
        "feedforward_bias": bell_draw(streams_of[11], (D,), 0.3, 1.5, ((0, 32),)),
        "inner_weight": bell_draw(streams_of[12], (D, FF), D ** -0.5, 0.21875, ((0, 32),)),
        "inner_bias": bell_draw(streams_of[13], (FF,), 0.3, 1.5, ((0, 32),)),
        "outer_weight": bell_draw(streams_of[14], (FF, D), FF ** -0.5, 0.109375, ((0, 32),)),
        "outer_bias": bell_draw(streams_of[15], (D,), 0.3, 1.5, ((0, 32),)),
        "cotangent": noise_with(streams_of[16], (SEQS, LEN, D), 1.0, 6.0, ((0, 8), (1, 4)), (0, 2, 8, 2.0)),
    }


@jax.custom_vjp
def low(v):
    return lax.optimization_barrier(v.astype(jnp.bfloat16)).astype(jnp.float32)

@jax.custom_vjp
def low_back(v):
    return v

def low_keep(v):
    return (low(v), None)

def low_pass(kept, grad):
    return (grad,)

def back_keep(v):
    return (v, None)

def back_low(kept, grad):
    return (low(grad),)
low.defvjp(low_keep, low_pass)
low_back.defvjp(back_keep, back_low)
HIGHEST = lax.Precision.HIGHEST
NEG_FILL = -1e+30
EPS_NORM = 1e-05

def product(left, right):
    return jnp.dot(left, right, precision=HIGHEST, preferred_element_type=jnp.float32)

def rotary_tables(positions):
    half_dims = ROT // 2
    inverse = 10000.0 ** (-jnp.arange(half_dims, dtype=jnp.float32) * 2.0 / ROT)
    angles = positions.astype(jnp.float32)[:, None] * inverse[None, :]
    return (jnp.cos(angles), jnp.sin(angles))

def rotate(features, cosine, sine_table):
    half_dims = ROT // 2
    first_half = features[..., :half_dims]
    second_half = features[..., half_dims:ROT]
    return jnp.concatenate([first_half * cosine - second_half * sine_table, second_half * cosine + first_half * sine_table, features[..., ROT:]], axis=-1)

def layer_forward(token_rows, parameters, cosine, sine_table, seq_len):
    attention_gain, attention_bias, query_weight, query_bias, keyvalue_weight, keyvalue_bias, output_weight, output_bias, feedforward_gain, feedforward_bias, inner_weight, inner_bias, outer_weight, outer_bias = parameters
    row_mean = lax.optimization_barrier(jnp.mean(token_rows, axis=-1, keepdims=True))
    centered = token_rows - row_mean
    normed = centered * lax.rsqrt(lax.optimization_barrier(jnp.mean(centered * centered, axis=-1, keepdims=True)) + EPS_NORM)
    attn_in = low(normed * attention_gain + attention_bias)
    query_lin = low_back(product(attn_in, query_weight) + query_bias).reshape(LEN, H, HS)
    query_used = low(rotate(query_lin, cosine[:, None, :], sine_table[:, None, :]) * HS ** (-0.5))
    keyvalue_lin = low_back(product(attn_in, keyvalue_weight) + keyvalue_bias)
    key_used = low(rotate(keyvalue_lin[:, :HS], cosine, sine_table))
    value_used = low(keyvalue_lin[:, HS:])
    row_span = min(512, LEN)
    key_index = jnp.arange(LEN).astype(jnp.int32)

    def query_rows(pieces):
        query_piece, offset = pieces
        query_index = offset + jnp.arange(row_span).astype(jnp.int32)
        scores = low_back(jnp.einsum('thd,kd->thk', query_piece, key_used, precision=HIGHEST))
        allowed = (key_index[None, :] <= query_index[:, None]) & (key_index[None, :] < seq_len)
        scores = jnp.where(allowed[:, None, :], scores, NEG_FILL)
        row_top = lax.optimization_barrier(jnp.max(scores, axis=-1, keepdims=True))
        exp_scores = jnp.exp(scores - row_top)
        probability = low(exp_scores / lax.optimization_barrier(jnp.sum(exp_scores, axis=-1, keepdims=True)))
        return jnp.einsum('thk,kd->thd', probability, value_used, precision=HIGHEST)
    offsets = (jnp.arange(LEN // row_span) * row_span).astype(jnp.int32)
    attn_mix = lax.map(jax.checkpoint(query_rows), (query_used.reshape(LEN // row_span, row_span, H, HS), offsets))
    attn_out = low(low_back(attn_mix.reshape(LEN, H * HS)))
    ff_in = low(normed * feedforward_gain + feedforward_bias)
    inner_pre = low_back(product(ff_in, inner_weight) + inner_bias)
    act_used = low(jax.nn.gelu(inner_pre, approximate=False))
    return token_rows + (product(attn_out, output_weight) + output_bias) + (product(act_used, outer_weight) + outer_bias)

def reference(tokens, seq_lengths, attention_gain, attention_bias, query_weight, query_bias, keyvalue_weight, keyvalue_bias, output_weight, output_bias, feedforward_gain, feedforward_bias, inner_weight, inner_bias, outer_weight, outer_bias, cotangent):
    parameters = tuple((tensor.astype(jnp.float32) for tensor in (attention_gain, attention_bias, query_weight, query_bias, keyvalue_weight, keyvalue_bias, output_weight, output_bias, feedforward_gain, feedforward_bias, inner_weight, inner_bias, outer_weight, outer_bias)))
    positions = jnp.arange(LEN).astype(jnp.int32)
    cosine, sine_table = rotary_tables(positions)

    def per_sequence(totals, seq_items):
        seq_tokens, seq_len, seq_cot = seq_items
        live_rows = (positions < seq_len)[:, None]
        grad_out = jnp.where(live_rows, seq_cot.astype(jnp.float32), jnp.zeros((), jnp.float32))

        def forward(token_rows, *weights):
            return layer_forward(token_rows, weights, cosine, sine_table, seq_len)
        result, pullback = jax.vjp(forward, seq_tokens.astype(jnp.float32), *parameters)
        all_grads = pullback(grad_out)
        totals = jax.tree.map(jnp.add, totals, tuple(all_grads[1:]))
        return (totals, (result.astype(jnp.bfloat16), all_grads[0]))
    zero_grads = tuple((jnp.zeros_like(tensor) for tensor in parameters))
    totals, (outputs, token_grads) = lax.scan(per_sequence, zero_grads, (tokens, seq_lengths, cotangent))
    return (outputs, token_grads, totals[0], totals[1], totals[2], totals[3], totals[4], totals[5], totals[6], totals[7], totals[8], totals[9], totals[10], totals[11], totals[12], totals[13])
```

```python
import functools

import jax
import jax.numpy as jnp
from jax import lax
from jax.experimental import pallas as pl
from jax.experimental.pallas import tpu as pltpu
from jax.sharding import PartitionSpec as P

ROT = 16
NEG_FILL = -1e30
EPS_NORM = 1e-05
ROOT_HALF = 0.7071067811865476
INV_ROOT_TAU = 0.3989422804014327
AXES = ("dp", "ctx")
BF = jnp.bfloat16
F32 = jnp.float32
VMEM_LIMIT = 56 * 1024 * 1024

ERFC_P = 0.4
ERFC_Q = (
    0.22562630138784126,
    0.22657565341595295,
    0.20095899601354286,
    0.19696137863906577,
    0.07151224850837805,
    0.09972378555265057,
    0.07384727992427025,
    -0.13547360511236364,
    0.040268019251938104,
)


def dot(a, b):
    return lax.dot_general(a, b, (((1,), (0,)), ((), ())), preferred_element_type=F32)


def dot_nt(a, b):
    return lax.dot_general(a, b, (((1,), (1,)), ((), ())), preferred_element_type=F32)


def dot_tn(a, b):
    return lax.dot_general(a, b, (((0,), (0,)), ((), ())), preferred_element_type=F32)


def row_norm(x):
    mean = jnp.mean(x, axis=-1, keepdims=True)
    centered = x - mean
    inverse = lax.rsqrt(jnp.mean(centered * centered, axis=-1, keepdims=True) + EPS_NORM)
    return centered * inverse, inverse


def gelu_parts(u):
    z = jnp.abs(u) * ROOT_HALF
    t = 1.0 / (1.0 + ERFC_P * z)
    poly = jnp.full_like(t, ERFC_Q[-1])
    for coefficient in ERFC_Q[-2::-1]:
        poly = poly * t + coefficient
    bell = jnp.exp(-0.5 * u * u)
    tail = 0.5 * bell * (t * poly)
    return jnp.where(u >= 0.0, 1.0 - tail, tail), u * bell * INV_ROOT_TAU


def rotary_planes(positions, head_size):
    lane = jnp.arange(128, dtype=jnp.int32) % head_size
    half = ROT // 2
    inverse = 10000.0 ** (-(lane % half).astype(F32) * 2.0 / ROT)
    angles = positions.astype(F32)[:, None] * inverse[None, :]
    lane = lane[None, :]
    cosine = jnp.where(lane < ROT, jnp.cos(angles), 1.0)
    sine = jnp.sin(angles)
    upper = jnp.where(lane < half, -sine, 0.0)
    lower = jnp.where((lane >= half) & (lane < ROT), sine, 0.0)
    return cosine, upper, lower


def turn(x, cosine, upper, lower):
    half = ROT // 2
    return x * cosine + pltpu.roll(x, 128 - half, 1) * upper + pltpu.roll(x, half, 1) * lower


def keyvalue_kernel(tok, gain, bias, weight, kv_bias, cos, up, low, attn_in_ref, kv_ref):
    normed, _ = row_norm(tok[...].astype(F32))
    attn_in = (normed * gain[...] + bias[...]).astype(BF)
    attn_in_ref[...] = attn_in
    lin = dot(attn_in, weight[...]) + kv_bias[...]
    lane = lax.broadcasted_iota(jnp.int32, lin.shape, 1)
    turned = turn(lin, cos[...], up[...], low[...])
    kv_ref[...] = jnp.where(lane < 64, turned, lin).astype(BF)


def keyvalue_project(tokens, gain, bias, weight, kv_bias, planes, block):
    rows, width = tokens.shape
    local_len = planes[0].shape[0]
    per_seq = local_len // block
    row_spec = lambda cols: pl.BlockSpec((block, cols), lambda i: (i, 0))
    full = lambda shape: pl.BlockSpec(shape, lambda i: (0, 0))
    plane = pl.BlockSpec((block, 128), lambda i: (i % per_seq, 0))
    return pl.pallas_call(
        keyvalue_kernel,
        grid=(rows // block,),
        in_specs=[row_spec(width), full((1, width)), full((1, width)), full(weight.shape), full((1, 128))]
        + [plane] * 3,
        out_specs=[row_spec(width), row_spec(128)],
        out_shape=[jax.ShapeDtypeStruct((rows, width), BF), jax.ShapeDtypeStruct((rows, 128), BF)],
        compiler_params=pltpu.CompilerParams(vmem_limit_bytes=VMEM_LIMIT),
        cost_estimate=pl.CostEstimate(
            flops=2 * rows * width * 128, transcendentals=rows, bytes_accessed=rows * width * 4
        ),
        name="keyvalue_project",
    )(tokens, gain, bias, weight, kv_bias, *planes)


def query_kernel(block, per_seq, scalars, attn_in, cot, weight, q_bias, out_weight, cos, up, low, q_ref, mg_ref):
    step = pl.program_id(0)
    width = attn_in.shape[1]
    lin = dot(attn_in[...], weight[...]) + q_bias[...]
    scale = 64 ** (-0.5)
    for pair in range(width // 128):
        lanes = slice(pair * 128, (pair + 1) * 128)
        q_ref[:, lanes] = (turn(lin[:, lanes], cos[...], up[...], low[...]) * scale).astype(BF)
    start = scalars[0] + lax.rem(step, per_seq) * block
    position = start + lax.broadcasted_iota(jnp.int32, (block, 1), 0)
    live = position < scalars[1 + step // per_seq]
    grad = jnp.where(live, cot[...].astype(F32), 0.0).astype(BF)
    mg_ref[...] = dot_nt(grad, out_weight[...]).astype(BF)


def query_project(scalars, attn_in, cot, weight, q_bias, out_weight, planes, block):
    rows, width = attn_in.shape
    local_len = planes[0].shape[0]
    per_seq = local_len // block
    row_spec = pl.BlockSpec((block, width), lambda i, s: (i, 0))
    full = lambda shape: pl.BlockSpec(shape, lambda i, s: (0, 0))
    plane = pl.BlockSpec((block, 128), lambda i, s: (i % per_seq, 0))
    return pl.pallas_call(
        functools.partial(query_kernel, block, per_seq),
        grid_spec=pltpu.PrefetchScalarGridSpec(
            num_scalar_prefetch=1,
            grid=(rows // block,),
            in_specs=[row_spec, row_spec, full(weight.shape), full((1, width)), full(out_weight.shape)]
            + [plane] * 3,
            out_specs=[row_spec, row_spec],
        ),
        out_shape=[jax.ShapeDtypeStruct((rows, width), BF)] * 2,
        compiler_params=pltpu.CompilerParams(vmem_limit_bytes=VMEM_LIMIT),
        cost_estimate=pl.CostEstimate(
            flops=4 * rows * width * width, transcendentals=0, bytes_accessed=rows * width * 8 + width * width * 4
        ),
        name="query_project",
    )(scalars, attn_in, cot, weight, q_bias, out_weight, *planes)


def attention_kernel(
    chunk, scalars, q_ref, mg_ref, kv_ref, cos, up, low, o_ref, qg_ref, dkv_ref,
    key0, key1, val0, val1, sc, dps, acc_k, acc_v,
):
    step = pl.program_id(0)
    offset, seq_len = scalars[0], scalars[1]
    rows = q_ref.shape[0]
    total = kv_ref.shape[0]
    keys, vals = (key0, key1), (val0, val1)
    lane_small = lax.broadcasted_iota(jnp.int32, (1, 128), 1)
    left = lane_small < 64

    @pl.when(step == 0)
    def _():
        for start in range(0, total, chunk):
            part = pl.ds(start, chunk)
            kv = kv_ref[part, :].astype(F32)
            key_left = jnp.where(left, kv, 0.0)
            val_right = jnp.where(left, 0.0, kv)
            key0[part, :] = key_left.astype(BF)
            key1[part, :] = pltpu.roll(key_left, 64, 1).astype(BF)
            val1[part, :] = val_right.astype(BF)
            val0[part, :] = pltpu.roll(val_right, 64, 1).astype(BF)
            acc_k[part, :] = jnp.zeros((chunk, 128), F32)
            acc_v[part, :] = jnp.zeros((chunk, 128), F32)

    last = jnp.minimum(offset + rows, seq_len)
    count = (last + chunk - 1) // chunk
    whole = jnp.minimum(offset, seq_len) // chunk
    query = q_ref[...]
    mix_grad = mg_ref[...]

    def score_step(masked, index, tops):
        part = pl.ds(pl.multiple_of(index * chunk, chunk), chunk)
        fresh = []
        for head in range(2):
            scores = dot_nt(query, keys[head][part, :])
            if masked:
                row = offset + lax.broadcasted_iota(jnp.int32, scores.shape, 0)
                col = index * chunk + lax.broadcasted_iota(jnp.int32, scores.shape, 1)
                scores = jnp.where((col <= row) & (col < seq_len), scores, NEG_FILL)
            sc[head, index] = scores
            fresh.append(jnp.maximum(tops[head], jnp.max(scores, axis=1, keepdims=True)))
        return tuple(fresh)

    low_top = jnp.full((rows, 1), NEG_FILL, F32)
    tops = lax.fori_loop(0, whole, functools.partial(score_step, False), (low_top, low_top))
    tops = lax.fori_loop(whole, count, functools.partial(score_step, True), tops)

    def mix_step(backward, index, state):
        part = pl.ds(pl.multiple_of(index * chunk, chunk), chunk)
        mix, sums, dots = state
        new_sums, new_dots = [], []
        for head in range(2):
            weights = jnp.exp(sc[head, index] - tops[head])
            sc[head, index] = weights
            new_sums.append(sums[head] + jnp.sum(weights, axis=1, keepdims=True))
            mix = mix + dot(weights.astype(BF), vals[head][part, :])
            if backward:
                prob_grad = dot_nt(mix_grad, vals[head][part, :])
                dps[head, index] = prob_grad
                new_dots.append(dots[head] + jnp.sum(weights * prob_grad, axis=1, keepdims=True))
            else:
                new_dots.append(dots[head])
        return mix, tuple(new_sums), tuple(new_dots)

    zero_col = jnp.zeros((rows, 1), F32)
    start_state = (jnp.zeros((rows, 128), F32), (zero_col, zero_col), (zero_col, zero_col))

    def finish_mix(mix, sums):
        inverses = (1.0 / sums[0], 1.0 / sums[1])
        spread = jnp.where(left, inverses[0], inverses[1])
        o_ref[...] = (mix * spread).astype(BF)
        return inverses, spread

    @pl.when(offset >= seq_len)
    def _():
        mix, sums, _ = lax.fori_loop(0, count, functools.partial(mix_step, False), start_state)
        finish_mix(mix, sums)
        qg_ref[...] = jnp.zeros(qg_ref.shape, BF)

    @pl.when(offset < seq_len)
    def _():
        mix, sums, dots = lax.fori_loop(0, count, functools.partial(mix_step, True), start_state)
        inverses, spread = finish_mix(mix, sums)
        dots = (dots[0] * inverses[0], dots[1] * inverses[1])
        query_f = query.astype(F32) * spread
        mix_grad_f = mix_grad.astype(F32) * spread
        query_own = (jnp.where(left, query_f, 0.0).astype(BF), jnp.where(left, 0.0, query_f).astype(BF))
        grad_own = (jnp.where(left, mix_grad_f, 0.0).astype(BF), jnp.where(left, 0.0, mix_grad_f).astype(BF))

        def grad_step(index, query_grad):
            part = pl.ds(pl.multiple_of(index * chunk, chunk), chunk)
            new_k = acc_k[part, :]
            new_v = acc_v[part, :]
            for head in range(2):
                weights = sc[head, index]
                score_grad = (weights * (dps[head, index] - dots[head])).astype(BF)
                query_grad = query_grad + dot(score_grad, keys[head][part, :])
                new_k = new_k + dot_tn(score_grad, query_own[head])
                new_v = new_v + dot_tn(weights.astype(BF), grad_own[head])
            acc_k[part, :] = new_k
            acc_v[part, :] = new_v
            return query_grad

        query_grad = lax.fori_loop(0, count, grad_step, jnp.zeros((rows, 128), F32))
        query_grad = query_grad * (spread * 64 ** (-0.5))
        qg_ref[...] = turn(query_grad, cos[...], -up[...], -low[...]).astype(BF)

    @pl.when(step == pl.num_programs(0) - 1)
    def _():
        for start in range(0, total, chunk):
            part = pl.ds(start, chunk)
            key_sum = acc_k[part, :]
            val_sum = acc_v[part, :]
            key_sum = key_sum + pltpu.roll(key_sum, 64, 1)
            val_sum = val_sum + pltpu.roll(val_sum, 64, 1)
            dkv_ref[part, :] = jnp.where(left, key_sum, val_sum)


def attention(scalars, q, mg, kv, planes, chunk):
    rows, width = q.shape
    total = kv.shape[0]
    pair = pl.BlockSpec((rows, 128), lambda i, s: (0, i))
    plane = pl.BlockSpec((rows, 128), lambda i, s: (0, 0))
    whole = pl.BlockSpec((total, 128), lambda i, s: (0, 0))
    heads = width // 64
    return pl.pallas_call(
        functools.partial(attention_kernel, chunk),
        grid_spec=pltpu.PrefetchScalarGridSpec(
            num_scalar_prefetch=1,
            grid=(width // 128,),
            in_specs=[pair, pair, whole] + [plane] * 3,
            out_specs=[pair, pair, whole],
            scratch_shapes=[pltpu.VMEM((total, 128), BF)] * 4
            + [pltpu.VMEM((2, total // chunk, rows, chunk), F32)] * 2
            + [pltpu.VMEM((total, 128), F32)] * 2,
        ),
        out_shape=[
            jax.ShapeDtypeStruct((rows, width), BF),
            jax.ShapeDtypeStruct((rows, width), BF),
            jax.ShapeDtypeStruct((total, 128), F32),
        ],
        compiler_params=pltpu.CompilerParams(vmem_limit_bytes=VMEM_LIMIT),
        cost_estimate=pl.CostEstimate(
            flops=12 * rows * heads * total * 256, transcendentals=rows * heads * total,
            bytes_accessed=rows * width * 8,
        ),
        name="attention",
    )(scalars, q, mg, kv, *planes)


def feed_kernel(
    block, local_len, scalars, tok, cot, gain, bias, inner, inner_bias, outer,
    y_ref, dff_ref, dinner_ref, douter_ref, dbias_ref, ff_in, grad, act, slope,
):
    step = pl.program_id(0)
    rows = tok.shape[0]
    spans = [pl.ds(start, block) for start in range(0, rows, block)]

    @pl.when(step == 0)
    def _():
        for number, span in enumerate(spans):
            normed, _ = row_norm(tok[span, :].astype(F32))
            ff_in[span, :] = (normed * gain[...] + bias[...]).astype(BF)
            start = number * block
            position = scalars[0] + start % local_len + lax.broadcasted_iota(jnp.int32, (block, 1), 0)
            live = position < scalars[1 + start // local_len]
            grad[span, :] = jnp.where(live, cot[span, :].astype(F32), 0.0).astype(BF)
            y_ref[span, :] = jnp.zeros((block, y_ref.shape[1]), F32)
            dff_ref[span, :] = jnp.zeros((block, y_ref.shape[1]), F32)

    bias_sum = jnp.zeros((1, inner.shape[1]), F32)
    for span in spans:
        pre = dot(ff_in[span, :], inner[...]) + inner_bias[...]
        back = dot_nt(grad[span, :], outer[...])
        share, density = gelu_parts(pre)
        act_part = (pre * share).astype(BF)
        slope_part = (back * (share + density)).astype(BF)
        act[span, :] = act_part
        slope[span, :] = slope_part
        bias_sum = bias_sum + jnp.sum(slope_part.astype(F32), axis=0, keepdims=True)
        y_ref[span, :] += dot(act_part, outer[...])
        dff_ref[span, :] += dot_nt(slope_part, inner[...])
    dbias_ref[...] = bias_sum
    dinner_ref[...] = dot_tn(ff_in[...], slope[...]).astype(BF)
    douter_ref[...] = dot_tn(act[...], grad[...]).astype(BF)


def feed_forward(scalars, tokens, cot, gain, bias, inner, inner_bias, outer, local_len, block, units):
    rows, width = tokens.shape
    hidden = inner.shape[1]
    full = lambda shape: pl.BlockSpec(shape, lambda i, s: (0, 0))
    return pl.pallas_call(
        functools.partial(feed_kernel, block, local_len),
        grid_spec=pltpu.PrefetchScalarGridSpec(
            num_scalar_prefetch=1,
            grid=(hidden // units,),
            in_specs=[
                full((rows, width)),
                full((rows, width)),
                full((1, width)),
                full((1, width)),
                pl.BlockSpec((width, units), lambda i, s: (0, i)),
                pl.BlockSpec((1, units), lambda i, s: (0, i)),
                pl.BlockSpec((units, width), lambda i, s: (i, 0)),
            ],
            out_specs=[
                full((rows, width)),
                full((rows, width)),
                pl.BlockSpec((width, units), lambda i, s: (0, i)),
                pl.BlockSpec((units, width), lambda i, s: (i, 0)),
                pl.BlockSpec((1, units), lambda i, s: (0, i)),
            ],
            scratch_shapes=[pltpu.VMEM((rows, width), BF)] * 2 + [pltpu.VMEM((rows, units), BF)] * 2,
        ),
        out_shape=[
            jax.ShapeDtypeStruct((rows, width), F32),
            jax.ShapeDtypeStruct((rows, width), F32),
            jax.ShapeDtypeStruct((width, hidden), BF),
            jax.ShapeDtypeStruct((hidden, width), BF),
            jax.ShapeDtypeStruct((1, hidden), F32),
        ],
        compiler_params=pltpu.CompilerParams(vmem_limit_bytes=VMEM_LIMIT),
        cost_estimate=pl.CostEstimate(
            flops=12 * rows * width * hidden, transcendentals=rows * hidden,
            bytes_accessed=rows * width * 12 + width * hidden * 8,
        ),
        name="feed_forward",
    )(scalars, tokens, cot, gain, bias, inner, inner_bias, outer)


def ring_gather(piece, context_index):
    count = lax.axis_size("ctx")
    rows = piece.shape[0]
    whole = jnp.zeros((count * rows, piece.shape[1]), piece.dtype)
    whole = lax.dynamic_update_slice_in_dim(whole, piece, context_index * rows, 0)
    for distance in range(1, count):
        arrived = lax.ppermute(piece, "ctx", [(i, (i + distance) % count) for i in range(count)])
        source = lax.rem(context_index - distance + count, count)
        whole = lax.dynamic_update_slice_in_dim(whole, arrived, source * rows, 0)
    return whole


def ring_scatter_sum(whole, context_index):
    count = lax.axis_size("ctx")
    rows = whole.shape[0] // count
    total = lax.dynamic_slice_in_dim(whole, context_index * rows, rows, 0)
    for distance in range(1, count):
        target = lax.rem(context_index + distance, count)
        piece = lax.dynamic_slice_in_dim(whole, target * rows, rows, 0).astype(BF)
        arrived = lax.ppermute(piece, "ctx", [(i, (i + distance) % count) for i in range(count)])
        total = total + arrived.astype(F32)
    return total


def sum_everywhere(x):
    for axis in ("dp", "ctx"):
        size = lax.axis_size(axis)
        bit = 1
        while bit < size:
            x = x + lax.ppermute(x, axis, [(i, i ^ bit) for i in range(size)])
            bit *= 2
    return x


def local(
    tokens,
    seq_lengths,
    attention_gain,
    attention_bias,
    query_weight,
    query_bias,
    keyvalue_weight,
    keyvalue_bias,
    output_weight,
    output_bias,
    feedforward_gain,
    feedforward_bias,
    inner_weight,
    inner_bias,
    outer_weight,
    outer_bias,
    cotangent,
):
    seqs, local_len, width = tokens.shape
    head_size = keyvalue_weight.shape[1] // 2
    rows = seqs * local_len
    shard = query_weight.shape[0]
    hidden = inner_weight.shape[1]
    context_index = lax.axis_index("ctx")
    device_index = lax.axis_index("dp") * lax.axis_size("ctx") + context_index
    block = min(256, local_len)
    chunk = min(512, local_len)
    offset = context_index * local_len
    position = offset + jnp.arange(local_len, dtype=jnp.int32)
    planes = rotary_planes(position, head_size)
    scalars = jnp.concatenate([offset[None].astype(jnp.int32), seq_lengths])
    tok = tokens.reshape(rows, width)
    cot = cotangent.reshape(rows, width)

    vectors = [attention_gain, attention_bias, feedforward_gain, feedforward_bias, query_bias, output_bias, outer_bias]
    side = jnp.stack(vectors, axis=1)
    side = jnp.concatenate([side, inner_bias.reshape(shard, -1)], axis=1)
    side = jnp.pad(side, ((0, 0), (0, 128 - side.shape[1])))
    packed = jnp.concatenate([query_weight, output_weight, keyvalue_weight, side], axis=1)
    packed = lax.all_gather(packed, AXES, axis=0, tiled=True)
    query_full = packed[:, :width]
    output_full = packed[:, width : 2 * width]
    keyvalue_full = packed[:, 2 * width : 2 * width + 128]
    side = packed[:, 2 * width + 128 :].astype(F32)
    gain_attn, bias_attn, gain_ff, bias_ff, q_shift, o_shift, outer_shift = [side[:, i][None, :] for i in range(7)]
    inner_shift = side[:, 7 : 7 + hidden // width].reshape(1, hidden)
    inner_full = lax.all_gather(inner_weight, AXES, axis=0, tiled=True)
    outer_full = lax.all_gather(outer_weight, AXES, axis=0, tiled=True)
    kv_shift = keyvalue_bias.astype(F32)[None, :]

    attn_in, kv_own = keyvalue_project(tok, gain_attn, bias_attn, keyvalue_full, kv_shift, planes, block)
    kv_all = [ring_gather(kv_own[s * local_len : (s + 1) * local_len], context_index) for s in range(seqs)]
    q, mg = query_project(scalars, attn_in, cot, query_full, q_shift, output_full, planes, block)

    def attend(s):
        part = slice(s * local_len, (s + 1) * local_len)
        own = jnp.stack([scalars[0], scalars[1 + s]])
        return attention(own, q[part], mg[part], kv_all[s], planes, chunk)

    results = [attend(s) for s in range(seqs)]
    y_ff, ff_in_grad, inner_grad_w, outer_grad_w, inner_grad_b = feed_forward(
        scalars, tok, cot, gain_ff, bias_ff, inner_full, inner_shift, outer_full, local_len, block, min(256, hidden)
    )
    attn_out = jnp.concatenate([r[0] for r in results])
    query_lin_grad = jnp.concatenate([r[1] for r in results])
    kv_grad = jnp.concatenate([ring_scatter_sum(r[2], context_index) for r in results])

    cosine, upper, lower = [jnp.tile(p, (seqs, 1)) for p in planes]
    lane = jnp.arange(128)[None, :]
    half = ROT // 2
    kv_grad = kv_grad.astype(BF).astype(F32)
    turned = kv_grad * cosine - jnp.roll(kv_grad, -half, 1) * upper - jnp.roll(kv_grad, half, 1) * lower
    kv_lin_grad = jnp.where(lane < head_size, turned, kv_grad).astype(BF)

    live = (position[None, :] < seq_lengths[:, None]).reshape(rows, 1)
    grad_out = jnp.where(live, cot, jnp.zeros((), BF))
    grad_float = grad_out.astype(F32)
    token_rows = tok.astype(F32)
    normed, inverse = row_norm(token_rows)

    outputs = token_rows + (dot(attn_out, output_full) + o_shift) + (y_ff + outer_shift)
    outputs = outputs.astype(BF)

    query_grad_w = dot_tn(attn_in, query_lin_grad)
    output_grad_w = dot_tn(attn_out, grad_out)
    kv_grad_w = dot_tn(attn_in, kv_lin_grad)
    attn_in_grad = dot_nt(query_lin_grad, query_full) + dot_nt(kv_lin_grad, keyvalue_full)

    branch = jnp.sum(grad_float, axis=0)
    small = jnp.concatenate(
        [
            jnp.sum(attn_in_grad * normed, axis=0),
            jnp.sum(attn_in_grad, axis=0),
            jnp.sum(ff_in_grad * normed, axis=0),
            jnp.sum(ff_in_grad, axis=0),
            jnp.sum(query_lin_grad.astype(F32), axis=0),
            branch,
            inner_grad_b[0],
            jnp.sum(kv_lin_grad.astype(F32), axis=0),
        ]
    )
    normed_grad = attn_in_grad * gain_attn + ff_in_grad * gain_ff
    centered = (
        normed_grad
        - jnp.mean(normed_grad, axis=-1, keepdims=True)
        - normed * jnp.mean(normed_grad * normed, axis=-1, keepdims=True)
    )
    token_grads = grad_float + inverse * centered

    attn_grads = jnp.concatenate([query_grad_w, output_grad_w, kv_grad_w], axis=1).astype(BF)
    scatter = lambda x: lax.psum_scatter(x, AXES, scatter_dimension=0, tiled=True).astype(F32)
    inner_shard = scatter(inner_grad_w)
    outer_shard = scatter(outer_grad_w)
    attn_shard = scatter(attn_grads)
    small = sum_everywhere(small.reshape(-1, 128)).reshape(-1)

    def own(index):
        return lax.dynamic_slice_in_dim(small, index * width + device_index * shard, shard)

    inner_own = hidden * shard // width
    bi = lax.dynamic_slice_in_dim(small, 6 * width + device_index * inner_own, inner_own)
    kvb = small[6 * width + hidden :]
    return (
        outputs.reshape(tokens.shape),
        token_grads.reshape(tokens.shape),
        own(0),
        own(1),
        attn_shard[:, :width],
        own(4),
        attn_shard[:, 2 * width :],
        kvb,
        attn_shard[:, width : 2 * width],
        own(5),
        own(2),
        own(3),
        inner_shard,
        bi,
        outer_shard,
        own(5),
    )


def solution(mesh):
    shard = P(("dp", "ctx"))
    matrix = P(("dp", "ctx"), None)
    token = P("dp", "ctx", None)
    in_specs = (
        token, P("dp"), shard, shard, matrix, shard, matrix, P(), matrix, shard,
        shard, shard, matrix, shard, matrix, shard, token,
    )
    out_specs = (
        token, token, shard, shard, matrix, shard, matrix, P(), matrix, shard,
        shard, shard, matrix, shard, matrix, shard,
    )
    return jax.shard_map(local, mesh=mesh, in_specs=in_specs, out_specs=out_specs, check_vma=False)
```

```python
import functools

import jax
import jax.numpy as jnp
from jax import lax
from jax.experimental import pallas as pl
from jax.experimental.pallas import tpu as pltpu
from jax.sharding import PartitionSpec as P

ROT = 16
NEG_FILL = -1e30
EPS_NORM = 1e-05
ROOT_HALF = 0.7071067811865476
INV_ROOT_TAU = 0.3989422804014327
AXES = ("dp", "ctx")
BF = jnp.bfloat16
F32 = jnp.float32
VMEM_LIMIT = 56 * 1024 * 1024

ERFC_P = 0.4
ERFC_Q = (
    0.22562630138784126,
    0.22657565341595295,
    0.20095899601354286,
    0.19696137863906577,
    0.07151224850837805,
    0.09972378555265057,
    0.07384727992427025,
    -0.13547360511236364,
    0.040268019251938104,
)


def dot(a, b):
    return lax.dot_general(a, b, (((1,), (0,)), ((), ())), preferred_element_type=F32)


def dot_nt(a, b):
    return lax.dot_general(a, b, (((1,), (1,)), ((), ())), preferred_element_type=F32)


def dot_tn(a, b):
    return lax.dot_general(a, b, (((0,), (0,)), ((), ())), preferred_element_type=F32)


def row_norm(x):
    mean = jnp.mean(x, axis=-1, keepdims=True)
    centered = x - mean
    inverse = lax.rsqrt(jnp.mean(centered * centered, axis=-1, keepdims=True) + EPS_NORM)
    return centered * inverse, inverse


def gelu_parts(u):
    z = jnp.abs(u) * ROOT_HALF
    t = 1.0 / (1.0 + ERFC_P * z)
    poly = jnp.full_like(t, ERFC_Q[-1])
    for coefficient in ERFC_Q[-2::-1]:
        poly = poly * t + coefficient
    bell = jnp.exp(-0.5 * u * u)
    tail = 0.5 * bell * (t * poly)
    return jnp.where(u >= 0.0, 1.0 - tail, tail), u * bell * INV_ROOT_TAU


def rotary_planes(positions, head_size):
    lane = jnp.arange(128, dtype=jnp.int32) % head_size
    half = ROT // 2
    inverse = 10000.0 ** (-(lane % half).astype(F32) * 2.0 / ROT)
    angles = positions.astype(F32)[:, None] * inverse[None, :]
    lane = lane[None, :]
    cosine = jnp.where(lane < ROT, jnp.cos(angles), 1.0)
    sine = jnp.sin(angles)
    upper = jnp.where(lane < half, -sine, 0.0)
    lower = jnp.where((lane >= half) & (lane < ROT), sine, 0.0)
    return cosine, upper, lower


def turn(x, cosine, upper, lower):
    half = ROT // 2
    return x * cosine + pltpu.roll(x, 128 - half, 1) * upper + pltpu.roll(x, half, 1) * lower


def keyvalue_kernel(tok, gain, bias, weight, kv_bias, cos, up, low, attn_in_ref, kv_ref):
    normed, _ = row_norm(tok[...].astype(F32))
    attn_in = (normed * gain[...] + bias[...]).astype(BF)
    attn_in_ref[...] = attn_in
    lin = dot(attn_in, weight[...]) + kv_bias[...]
    lane = lax.broadcasted_iota(jnp.int32, lin.shape, 1)
    turned = turn(lin, cos[...], up[...], low[...])
    kv_ref[...] = jnp.where(lane < 64, turned, lin).astype(BF)


def keyvalue_project(tokens, gain, bias, weight, kv_bias, planes, block):
    rows, width = tokens.shape
    local_len = planes[0].shape[0]
    per_seq = local_len // block
    row_spec = lambda cols: pl.BlockSpec((block, cols), lambda i: (i, 0))
    full = lambda shape: pl.BlockSpec(shape, lambda i: (0, 0))
    plane = pl.BlockSpec((block, 128), lambda i: (i % per_seq, 0))
    return pl.pallas_call(
        keyvalue_kernel,
        grid=(rows // block,),
        in_specs=[row_spec(width), full((1, width)), full((1, width)), full(weight.shape), full((1, 128))]
        + [plane] * 3,
        out_specs=[row_spec(width), row_spec(128)],
        out_shape=[jax.ShapeDtypeStruct((rows, width), BF), jax.ShapeDtypeStruct((rows, 128), BF)],
        compiler_params=pltpu.CompilerParams(vmem_limit_bytes=VMEM_LIMIT),
        cost_estimate=pl.CostEstimate(
            flops=2 * rows * width * 128, transcendentals=rows, bytes_accessed=rows * width * 4
        ),
        name="keyvalue_project",
    )(tokens, gain, bias, weight, kv_bias, *planes)


def query_kernel(block, per_seq, scalars, attn_in, cot, weight, q_bias, out_weight, cos, up, low, q_ref, mg_ref):
    step = pl.program_id(0)
    width = attn_in.shape[1]
    lin = dot(attn_in[...], weight[...]) + q_bias[...]
    scale = 64 ** (-0.5)
    for pair in range(width // 128):
        lanes = slice(pair * 128, (pair + 1) * 128)
        q_ref[:, lanes] = (turn(lin[:, lanes], cos[...], up[...], low[...]) * scale).astype(BF)
    start = scalars[0] + lax.rem(step, per_seq) * block
    position = start + lax.broadcasted_iota(jnp.int32, (block, 1), 0)
    live = position < scalars[1 + step // per_seq]
    grad = jnp.where(live, cot[...].astype(F32), 0.0).astype(BF)
    mg_ref[...] = dot_nt(grad, out_weight[...]).astype(BF)


def query_project(scalars, attn_in, cot, weight, q_bias, out_weight, planes, block):
    rows, width = attn_in.shape
    local_len = planes[0].shape[0]
    per_seq = local_len // block
    row_spec = pl.BlockSpec((block, width), lambda i, s: (i, 0))
    full = lambda shape: pl.BlockSpec(shape, lambda i, s: (0, 0))
    plane = pl.BlockSpec((block, 128), lambda i, s: (i % per_seq, 0))
    return pl.pallas_call(
        functools.partial(query_kernel, block, per_seq),
        grid_spec=pltpu.PrefetchScalarGridSpec(
            num_scalar_prefetch=1,
            grid=(rows // block,),
            in_specs=[row_spec, row_spec, full(weight.shape), full((1, width)), full(out_weight.shape)]
            + [plane] * 3,
            out_specs=[row_spec, row_spec],
        ),
        out_shape=[jax.ShapeDtypeStruct((rows, width), BF)] * 2,
        compiler_params=pltpu.CompilerParams(vmem_limit_bytes=VMEM_LIMIT),
        cost_estimate=pl.CostEstimate(
            flops=4 * rows * width * width, transcendentals=0, bytes_accessed=rows * width * 8 + width * width * 4
        ),
        name="query_project",
    )(scalars, attn_in, cot, weight, q_bias, out_weight, *planes)


def attention_kernel(
    chunk, pieces, scalars, q_ref, mg_ref, *refs
):
    kv_refs, refs = refs[:pieces], refs[pieces:]
    (cos, up, low, o_ref, qg_ref), refs = refs[:5], refs[5:]
    dkv_refs, refs = refs[:pieces], refs[pieces:]
    key0, key1, val0, val1, sc, dps, acc_k, acc_v = refs
    step = pl.program_id(0)
    offset, seq_len, index = scalars[0], scalars[1], scalars[2]
    rows = q_ref.shape[0]
    span = kv_refs[0].shape[0]
    keys, vals = (key0, key1), (val0, val1)
    lane_small = lax.broadcasted_iota(jnp.int32, (1, 128), 1)
    left = lane_small < 64

    @pl.when(step == 0)
    def _():
        for distance in range(pieces):
            source = lax.rem(index + (pieces - distance), pieces)
            part = pl.ds(pl.multiple_of(source * span, span), span)
            kv = kv_refs[distance][...].astype(F32)
            key_left = jnp.where(left, kv, 0.0)
            val_right = jnp.where(left, 0.0, kv)
            key0[part, :] = key_left.astype(BF)
            key1[part, :] = pltpu.roll(key_left, 64, 1).astype(BF)
            val1[part, :] = val_right.astype(BF)
            val0[part, :] = pltpu.roll(val_right, 64, 1).astype(BF)
            acc_k[part, :] = jnp.zeros((span, 128), F32)
            acc_v[part, :] = jnp.zeros((span, 128), F32)

    last = jnp.minimum(offset + rows, seq_len)
    count = (last + chunk - 1) // chunk
    whole = jnp.minimum(offset, seq_len) // chunk
    query = q_ref[...]
    mix_grad = mg_ref[...]

    def score_step(masked, index, tops):
        part = pl.ds(pl.multiple_of(index * chunk, chunk), chunk)
        fresh = []
        for head in range(2):
            scores = dot_nt(query, keys[head][part, :])
            if masked:
                row = offset + lax.broadcasted_iota(jnp.int32, scores.shape, 0)
                col = index * chunk + lax.broadcasted_iota(jnp.int32, scores.shape, 1)
                scores = jnp.where((col <= row) & (col < seq_len), scores, NEG_FILL)
            sc[head, index] = scores
            fresh.append(jnp.maximum(tops[head], jnp.max(scores, axis=1, keepdims=True)))
        return tuple(fresh)

    low_top = jnp.full((rows, 1), NEG_FILL, F32)
    tops = lax.fori_loop(0, whole, functools.partial(score_step, False), (low_top, low_top))
    tops = lax.fori_loop(whole, count, functools.partial(score_step, True), tops)

    def mix_step(backward, index, state):
        part = pl.ds(pl.multiple_of(index * chunk, chunk), chunk)
        mix, sums, dots = state
        new_sums, new_dots = [], []
        for head in range(2):
            weights = jnp.exp(sc[head, index] - tops[head])
            sc[head, index] = weights
            new_sums.append(sums[head] + jnp.sum(weights, axis=1, keepdims=True))
            mix = mix + dot(weights.astype(BF), vals[head][part, :])
            if backward:
                prob_grad = dot_nt(mix_grad, vals[head][part, :])
                dps[head, index] = prob_grad
                new_dots.append(dots[head] + jnp.sum(weights * prob_grad, axis=1, keepdims=True))
            else:
                new_dots.append(dots[head])
        return mix, tuple(new_sums), tuple(new_dots)

    zero_col = jnp.zeros((rows, 1), F32)
    start_state = (jnp.zeros((rows, 128), F32), (zero_col, zero_col), (zero_col, zero_col))

    def finish_mix(mix, sums):
        inverses = (1.0 / sums[0], 1.0 / sums[1])
        spread = jnp.where(left, inverses[0], inverses[1])
        o_ref[...] = (mix * spread).astype(BF)
        return inverses, spread

    @pl.when(offset >= seq_len)
    def _():
        mix, sums, _ = lax.fori_loop(0, count, functools.partial(mix_step, False), start_state)
        finish_mix(mix, sums)
        qg_ref[...] = jnp.zeros(qg_ref.shape, BF)

    @pl.when(offset < seq_len)
    def _():
        mix, sums, dots = lax.fori_loop(0, count, functools.partial(mix_step, True), start_state)
        inverses, spread = finish_mix(mix, sums)
        dots = (dots[0] * inverses[0], dots[1] * inverses[1])
        query_f = query.astype(F32) * spread
        mix_grad_f = mix_grad.astype(F32) * spread
        query_own = (jnp.where(left, query_f, 0.0).astype(BF), jnp.where(left, 0.0, query_f).astype(BF))
        grad_own = (jnp.where(left, mix_grad_f, 0.0).astype(BF), jnp.where(left, 0.0, mix_grad_f).astype(BF))

        def grad_step(index, query_grad):
            part = pl.ds(pl.multiple_of(index * chunk, chunk), chunk)
            new_k = acc_k[part, :]
            new_v = acc_v[part, :]
            for head in range(2):
                weights = sc[head, index]
                score_grad = (weights * (dps[head, index] - dots[head])).astype(BF)
                query_grad = query_grad + dot(score_grad, keys[head][part, :])
                new_k = new_k + dot_tn(score_grad, query_own[head])
                new_v = new_v + dot_tn(weights.astype(BF), grad_own[head])
            acc_k[part, :] = new_k
            acc_v[part, :] = new_v
            return query_grad

        query_grad = lax.fori_loop(0, count, grad_step, jnp.zeros((rows, 128), F32))
        query_grad = query_grad * (spread * 64 ** (-0.5))
        qg_ref[...] = turn(query_grad, cos[...], -up[...], -low[...]).astype(BF)

    @pl.when(step == pl.num_programs(0) - 1)
    def _():
        for distance in range(pieces):
            owner = lax.rem(index + distance, pieces)
            part = pl.ds(pl.multiple_of(owner * span, span), span)
            key_sum = acc_k[part, :]
            val_sum = acc_v[part, :]
            key_sum = key_sum + pltpu.roll(key_sum, 64, 1)
            val_sum = val_sum + pltpu.roll(val_sum, 64, 1)
            dkv_refs[distance][...] = jnp.where(left, key_sum, val_sum).astype(dkv_refs[distance].dtype)


def attention(scalars, q, mg, seq, kv, planes, chunk):
    width = q.shape[1]
    pieces = len(kv)
    rows = span = kv[0].shape[0]
    total = span * pieces
    pair_in = pl.BlockSpec((rows, 128), lambda i, s: (seq, i))
    pair_out = pl.BlockSpec((rows, 128), lambda i, s: (0, i))
    plane = pl.BlockSpec((rows, 128), lambda i, s: (0, 0))
    heads = width // 64
    return pl.pallas_call(
        functools.partial(attention_kernel, chunk, pieces),
        grid_spec=pltpu.PrefetchScalarGridSpec(
            num_scalar_prefetch=1,
            grid=(width // 128,),
            in_specs=[pair_in, pair_in] + [plane] * (pieces + 3),
            out_specs=[pair_out, pair_out] + [plane] * pieces,
            scratch_shapes=[pltpu.VMEM((total, 128), BF)] * 4
            + [pltpu.VMEM((2, total // chunk, rows, chunk), F32)] * 2
            + [pltpu.VMEM((total, 128), F32)] * 2,
        ),
        out_shape=[jax.ShapeDtypeStruct((rows, width), BF)] * 2
        + [jax.ShapeDtypeStruct((span, 128), F32)]
        + [jax.ShapeDtypeStruct((span, 128), BF)] * (pieces - 1),
        compiler_params=pltpu.CompilerParams(vmem_limit_bytes=VMEM_LIMIT),
        cost_estimate=pl.CostEstimate(
            flops=12 * rows * heads * total * 256, transcendentals=rows * heads * total,
            bytes_accessed=rows * width * 8,
        ),
        name="attention",
    )(scalars, q, mg, *kv, *planes)


def feed_kernel(
    block, local_len, fold, scalars, tok, cot, side, inner, outer_rows, inner_bias,
    y_ref, dff_ref, grads_ref, dbias_ref, ff_in, grad, act, slope, outer,
):
    step = pl.program_id(0)
    rows, width = tok.shape
    units = inner.shape[1]
    part = units // fold
    spans = [pl.ds(start, block) for start in range(0, rows, block)]

    @pl.when(step == 0)
    def _():
        for number, span in enumerate(spans):
            normed, _ = row_norm(tok[span, :].astype(F32))
            ff_in[span, :] = (normed * side[2:3, :] + side[3:4, :]).astype(BF)
            start = number * block
            position = scalars[0] + start % local_len + lax.broadcasted_iota(jnp.int32, (block, 1), 0)
            live = position < scalars[1 + start // local_len]
            grad[span, :] = jnp.where(live, cot[span, :].astype(F32), 0.0).astype(BF)
            y_ref[span, :] = jnp.zeros((block, width), F32)
            dff_ref[span, :] = jnp.zeros((block, width), F32)

    for j in range(fold):
        outer[j * part : (j + 1) * part, :] = outer_rows[:, j * width : (j + 1) * width]
    bias_sum = jnp.zeros((1, units), F32)
    for span in spans:
        pre = dot(ff_in[span, :], inner[...]) + inner_bias[...]
        back = dot_nt(grad[span, :], outer[...])
        share, density = gelu_parts(pre)
        act_part = (pre * share).astype(BF)
        slope_part = (back * (share + density)).astype(BF)
        act[span, :] = act_part
        slope[span, :] = slope_part
        bias_sum = bias_sum + jnp.sum(slope_part.astype(F32), axis=0, keepdims=True)
        y_ref[span, :] += dot(act_part, outer[...])
        dff_ref[span, :] += dot_nt(slope_part, inner[...])
    dbias_ref[...] = bias_sum
    columns = pl.ds(pl.multiple_of(step * units, units), units)
    grads_ref[:, columns] = dot_tn(ff_in[...], slope[...]).astype(BF)
    douter = dot_tn(act[...], grad[...]).astype(BF)
    lines = pl.ds(pl.multiple_of(step * part, part), part)
    hidden = fold * width
    for j in range(fold):
        grads_ref[lines, hidden + j * width : hidden + (j + 1) * width] = douter[j * part : (j + 1) * part, :]


def feed_forward(scalars, tokens, cot, side, weights, inner_bias, local_len, block, units):
    rows, width = tokens.shape
    hidden = weights.shape[1] // 2
    fold = hidden // width
    one = pl.Buffered(1)
    full = lambda shape: pl.BlockSpec(shape, lambda i, s: (0, 0), pipeline_mode=one)
    return pl.pallas_call(
        functools.partial(feed_kernel, block, local_len, fold),
        grid_spec=pltpu.PrefetchScalarGridSpec(
            num_scalar_prefetch=1,
            grid=(hidden // units,),
            in_specs=[
                full((rows, width)),
                full((rows, width)),
                full(side.shape),
                pl.BlockSpec((width, units), lambda i, s: (0, i)),
                pl.BlockSpec((units // fold, hidden), lambda i, s: (i, 1)),
                pl.BlockSpec((1, units), lambda i, s: (0, i)),
            ],
            out_specs=[
                full((rows, width)),
                full((rows, width)),
                full((width, 2 * hidden)),
                pl.BlockSpec((1, units), lambda i, s: (0, i)),
            ],
            scratch_shapes=[pltpu.VMEM((rows, width), BF)] * 2
            + [pltpu.VMEM((rows, units), BF)] * 2
            + [pltpu.VMEM((units, width), BF)],
        ),
        out_shape=[
            jax.ShapeDtypeStruct((rows, width), F32),
            jax.ShapeDtypeStruct((rows, width), F32),
            jax.ShapeDtypeStruct((width, 2 * hidden), BF),
            jax.ShapeDtypeStruct((1, hidden), F32),
        ],
        compiler_params=pltpu.CompilerParams(vmem_limit_bytes=VMEM_LIMIT),
        cost_estimate=pl.CostEstimate(
            flops=12 * rows * width * hidden, transcendentals=rows * hidden,
            bytes_accessed=rows * width * 12 + width * hidden * 8,
        ),
        name="feed_forward",
    )(scalars, tokens, cot, side, weights, weights, inner_bias)


def shift_perm(distance, count):
    return [(i, (i + distance) % count) for i in range(count)]


def flip_perm(mask, count):
    return [(i, i ^ mask) for i in range(count)]


def dp_groups():
    bits = [1 << b for b in range((lax.axis_size("dp") - 1).bit_length())]
    rest = bits[1:]
    return [bits[:1]] + [rest[i : i + 2] for i in range(0, len(rest), 2)]


def combinations(bits):
    masks = [0]
    for bit in bits:
        masks += [m | bit for m in masks]
    return masks


def place_kernel(ways, count, key_counts, cuts, scalars, *refs):
    ins, outs = refs[: len(key_counts)], refs[len(key_counts) :]
    key = 0
    for ref, keys in zip(ins, key_counts):
        for slot in range(keys):
            for distance in range(count):
                source = lax.rem(scalars[1] + (count - distance), count)
                place = (scalars[0] ^ ways[key]) * count + source
                for out, start, end in zip(outs, cuts, cuts[1:]):
                    out[place] = ref[slot, distance, :, start:end]
            key += 1


def gather_all(x, cuts, dp_index, context_index):
    size, count = lax.axis_size("dp"), lax.axis_size("ctx")
    column = jnp.stack([x] + [lax.ppermute(x, "ctx", shift_perm(d, count)) for d in range(1, count)])
    stacks, ways = [column[None]], [0]
    for bits in reversed(dp_groups()):
        own = stacks[0] if len(stacks) == 1 else jnp.concatenate(stacks)
        arrived, new_ways = [], []
        for mask in combinations(bits)[1:]:
            arrived.append(lax.ppermute(own, "dp", flip_perm(mask, size)))
            new_ways += [w ^ mask for w in ways]
        stacks, ways = [own] + arrived, ways + new_ways
    return pl.pallas_call(
        functools.partial(place_kernel, ways, count, [s.shape[0] for s in stacks], cuts),
        grid_spec=pltpu.PrefetchScalarGridSpec(
            num_scalar_prefetch=1,
            grid=(1,),
            in_specs=[pl.BlockSpec(s.shape, lambda i, s: (0, 0, 0, 0)) for s in stacks],
            out_specs=[
                pl.BlockSpec((size * count, x.shape[0], e - b), lambda i, s: (0, 0, 0)) for b, e in zip(cuts, cuts[1:])
            ],
        ),
        out_shape=[jax.ShapeDtypeStruct((size * count, x.shape[0], e - b), x.dtype) for b, e in zip(cuts, cuts[1:])],
        compiler_params=pltpu.CompilerParams(vmem_limit_bytes=VMEM_LIMIT),
        name="place",
    )(jnp.stack([dp_index, context_index]), *stacks)


def scatter_sum(x, dp_index, context_index):
    size, count = lax.axis_size("dp"), lax.axis_size("ctx")
    x = x.reshape((size, count) + x.shape[1:])
    held = {key: lax.dynamic_index_in_dim(x, dp_index ^ key, 0, keepdims=False) for key in range(size)}
    for bits in dp_groups():
        masks = combinations(bits)
        keys = [k for k in held if not any(k & bit for bit in bits)]
        arrived = []
        for mask in masks[1:]:
            send = jnp.stack([held[k ^ mask].astype(BF) for k in keys])
            arrived.append(lax.ppermute(send, "dp", flip_perm(mask, size)))
        fresh = {}
        for slot, key in enumerate(keys):
            total = held[key].astype(F32)
            for part in arrived:
                total = total + part[slot].astype(F32)
            fresh[key] = total
        held = fresh
    column = held[0]
    total = lax.dynamic_index_in_dim(column, context_index, 0, keepdims=False)
    for distance in range(1, count):
        target = lax.rem(context_index + distance, count)
        piece = lax.dynamic_index_in_dim(column, target, 0, keepdims=False).astype(BF)
        total = total + lax.ppermute(piece, "ctx", shift_perm(distance, count)).astype(F32)
    return total


def sum_everywhere(x):
    for axis in ("dp", "ctx"):
        size = lax.axis_size(axis)
        bit = 1
        while bit < size:
            x = x + lax.ppermute(x, axis, flip_perm(bit, size))
            bit *= 2
    return x


def local(
    tokens,
    seq_lengths,
    attention_gain,
    attention_bias,
    query_weight,
    query_bias,
    keyvalue_weight,
    keyvalue_bias,
    output_weight,
    output_bias,
    feedforward_gain,
    feedforward_bias,
    inner_weight,
    inner_bias,
    outer_weight,
    outer_bias,
    cotangent,
):
    seqs, local_len, width = tokens.shape
    head_size = keyvalue_weight.shape[1] // 2
    rows = seqs * local_len
    shard = query_weight.shape[0]
    hidden = inner_weight.shape[1]
    context_index = lax.axis_index("ctx")
    count = lax.axis_size("ctx")
    device_index = lax.axis_index("dp") * count + context_index
    block = min(256, local_len)
    chunk = min(512, local_len)
    offset = context_index * local_len
    position = offset + jnp.arange(local_len, dtype=jnp.int32)
    planes = rotary_planes(position, head_size)
    scalars = jnp.concatenate([offset[None].astype(jnp.int32), seq_lengths])
    tok = tokens.reshape(rows, width)
    cot = cotangent.reshape(rows, width)

    dp_index = lax.axis_index("dp")
    devices = lax.axis_size("dp") * count
    vectors = [attention_gain, attention_bias, feedforward_gain, feedforward_bias, query_bias, output_bias, outer_bias]
    fold = hidden // width
    side = jnp.stack(vectors, axis=1)
    side = jnp.concatenate([side, inner_bias.reshape(shard, fold)], axis=1)
    side = jnp.pad(side, ((0, 0), (0, 128 - side.shape[1])))
    packed = jnp.concatenate([query_weight, output_weight, keyvalue_weight, side], axis=1)
    cuts = (0, width, 2 * width, 2 * width + 128, 2 * width + 256)
    gathered = gather_all(packed, cuts, dp_index, context_index)
    query_full, output_full, keyvalue_full, side = [g.reshape(width, -1) for g in gathered]
    side = side[:, :16].astype(F32).T
    gain_attn, bias_attn, gain_ff, bias_ff, q_shift, o_shift, outer_shift = [side[i : i + 1] for i in range(7)]

    units = min(768, hidden)
    owners = units // (fold * shard)

    def unit_order(x, back=False):
        sizes = (fold, owners) if back else (owners, fold)
        return x.reshape(x.shape[0], hidden // units, *sizes, shard).swapaxes(2, 3).reshape(x.shape[0], hidden)

    inner_shift = unit_order(side[7 : 7 + fold].T.reshape(1, hidden))
    late = outer_weight.reshape(fold, shard, width).swapaxes(0, 1).reshape(shard, hidden)
    late = lax.all_gather(jnp.concatenate([unit_order(inner_weight), late], axis=1), AXES, axis=0, tiled=True)
    kv_shift = keyvalue_bias.astype(F32)[None, :]

    attn_in, kv_own = keyvalue_project(tok, gain_attn, bias_attn, keyvalue_full, kv_shift, planes, block)
    q, mg = query_project(scalars, attn_in, cot, query_full, q_shift, output_full, planes, block)

    def attend(s, scalars):
        piece = kv_own[s * local_len : (s + 1) * local_len]
        pieces = [piece] + [lax.ppermute(piece, "ctx", shift_perm(d, count)) for d in range(1, count)]
        own = jnp.stack([scalars[0], scalars[1 + s], context_index])
        out, query_lin_grad, total, *others = attention(own, q, mg, s, pieces, planes, chunk)
        for distance, other in enumerate(others, 1):
            total = total + lax.ppermute(other, "ctx", shift_perm(distance, count)).astype(F32)
        return out, query_lin_grad, total

    results = [attend(0, scalars)]
    scalars_ff, _ = lax.optimization_barrier((scalars, results[0][0]))
    y_ff, ff_in_grad, late_grads, inner_grad_b = feed_forward(
        scalars_ff, tok, cot, side, late, inner_shift, local_len, block, units
    )
    inner_grad_b = unit_order(inner_grad_b, True)
    scalars_late, _ = lax.optimization_barrier((scalars, y_ff))
    results += [attend(s, scalars_late) for s in range(1, seqs)]
    attn_out = jnp.concatenate([r[0] for r in results])
    query_lin_grad = jnp.concatenate([r[1] for r in results])
    kv_grad = jnp.concatenate([r[2] for r in results])

    cosine, upper, lower = [jnp.tile(p, (seqs, 1)) for p in planes]
    lane = jnp.arange(128)[None, :]
    half = ROT // 2
    kv_grad = kv_grad.astype(BF).astype(F32)
    turned = kv_grad * cosine - jnp.roll(kv_grad, -half, 1) * upper - jnp.roll(kv_grad, half, 1) * lower
    kv_lin_grad = jnp.where(lane < head_size, turned, kv_grad).astype(BF)

    live = (position[None, :] < seq_lengths[:, None]).reshape(rows, 1)
    grad_out = jnp.where(live, cot, jnp.zeros((), BF))
    grad_float = grad_out.astype(F32)
    token_rows = tok.astype(F32)
    normed, inverse = row_norm(token_rows)

    outputs = token_rows + (dot(attn_out, output_full) + o_shift) + (y_ff + outer_shift)
    outputs = outputs.astype(BF)

    query_grad_w = dot_tn(attn_in, query_lin_grad)
    output_grad_w = dot_tn(attn_out, grad_out)
    kv_grad_w = dot_tn(attn_in, kv_lin_grad)
    attn_in_grad = dot_nt(query_lin_grad, query_full) + dot_nt(kv_lin_grad, keyvalue_full)

    branch = jnp.sum(grad_float, axis=0)
    small = jnp.concatenate(
        [
            jnp.sum(attn_in_grad * normed, axis=0),
            jnp.sum(attn_in_grad, axis=0),
            jnp.sum(ff_in_grad * normed, axis=0),
            jnp.sum(ff_in_grad, axis=0),
            jnp.sum(query_lin_grad.astype(F32), axis=0),
            branch,
            inner_grad_b[0],
            jnp.sum(kv_lin_grad.astype(F32), axis=0),
        ]
    )
    normed_grad = attn_in_grad * gain_attn + ff_in_grad * gain_ff
    centered = (
        normed_grad
        - jnp.mean(normed_grad, axis=-1, keepdims=True)
        - normed * jnp.mean(normed_grad * normed, axis=-1, keepdims=True)
    )
    token_grads = grad_float + inverse * centered

    blocks = lambda x: x.reshape(devices, shard, -1)
    late_shard = lax.psum_scatter(late_grads, AXES, scatter_dimension=0, tiled=True).astype(F32)
    inner_shard = unit_order(late_shard[:, :hidden], True)
    outer_shard = late_shard[:, hidden:].reshape(shard, fold, width).swapaxes(0, 1).reshape(-1, width)
    attn_shard = scatter_sum(blocks(jnp.concatenate([query_grad_w, output_grad_w], axis=1)), dp_index, context_index)
    kv_shard = scatter_sum(blocks(kv_grad_w), dp_index, context_index)
    small = sum_everywhere(small.reshape(-1, 128)).reshape(-1)

    def own(index):
        return lax.dynamic_slice_in_dim(small, index * width + device_index * shard, shard)

    inner_own = hidden * shard // width
    bi = lax.dynamic_slice_in_dim(small, 6 * width + device_index * inner_own, inner_own)
    kvb = small[6 * width + hidden :]
    return (
        outputs.reshape(tokens.shape),
        token_grads.reshape(tokens.shape),
        own(0),
        own(1),
        attn_shard[:, :width],
        own(4),
        kv_shard,
        kvb,
        attn_shard[:, width : 2 * width],
        own(5),
        own(2),
        own(3),
        inner_shard,
        bi,
        outer_shard,
        own(5),
    )


def solution(mesh):
    shard = P(("dp", "ctx"))
    matrix = P(("dp", "ctx"), None)
    token = P("dp", "ctx", None)
    in_specs = (
        token, P("dp"), shard, shard, matrix, shard, matrix, P(), matrix, shard,
        shard, shard, matrix, shard, matrix, shard, token,
    )
    out_specs = (
        token, token, shard, shard, matrix, shard, matrix, P(), matrix, shard,
        shard, shard, matrix, shard, matrix, shard,
    )
    return jax.shard_map(local, mesh=mesh, in_specs=in_specs, out_specs=out_specs, check_vma=False)
```

```python
import functools

import jax
import jax.numpy as jnp
from jax import lax
from jax.experimental import pallas as pl
from jax.experimental.pallas import tpu as pltpu
from jax.sharding import PartitionSpec as P

ROT = 16
NEG_FILL = -1e30
EPS_NORM = 1e-05
ROOT_HALF = 0.7071067811865476
INV_ROOT_TAU = 0.3989422804014327
AXES = ("dp", "ctx")
BF = jnp.bfloat16
F32 = jnp.float32
VMEM_LIMIT = 56 * 1024 * 1024

ERFC_P = 0.4
ERFC_Q = (
    0.22562630138784126,
    0.22657565341595295,
    0.20095899601354286,
    0.19696137863906577,
    0.07151224850837805,
    0.09972378555265057,
    0.07384727992427025,
    -0.13547360511236364,
    0.040268019251938104,
)


def dot(a, b):
    return lax.dot_general(a, b, (((1,), (0,)), ((), ())), preferred_element_type=F32)


def dot_nt(a, b):
    return lax.dot_general(a, b, (((1,), (1,)), ((), ())), preferred_element_type=F32)


def dot_tn(a, b):
    return lax.dot_general(a, b, (((0,), (0,)), ((), ())), preferred_element_type=F32)


def row_norm(x):
    mean = jnp.mean(x, axis=-1, keepdims=True)
    centered = x - mean
    inverse = lax.rsqrt(jnp.mean(centered * centered, axis=-1, keepdims=True) + EPS_NORM)
    return centered * inverse, inverse


def gelu_parts(u):
    z = jnp.abs(u) * ROOT_HALF
    t = 1.0 / (1.0 + ERFC_P * z)
    poly = jnp.full_like(t, ERFC_Q[-1])
    for coefficient in ERFC_Q[-2::-1]:
        poly = poly * t + coefficient
    bell = jnp.exp(-0.5 * u * u)
    tail = 0.5 * bell * (t * poly)
    return jnp.where(u >= 0.0, 1.0 - tail, tail), u * bell * INV_ROOT_TAU


def rotary_planes(positions, head_size):
    lane = jnp.arange(128, dtype=jnp.int32) % head_size
    half = ROT // 2
    inverse = 10000.0 ** (-(lane % half).astype(F32) * 2.0 / ROT)
    angles = positions.astype(F32)[:, None] * inverse[None, :]
    lane = lane[None, :]
    cosine = jnp.where(lane < ROT, jnp.cos(angles), 1.0)
    sine = jnp.sin(angles)
    upper = jnp.where(lane < half, -sine, 0.0)
    lower = jnp.where((lane >= half) & (lane < ROT), sine, 0.0)
    return cosine, upper, lower


def turn(x, cosine, upper, lower):
    half = ROT // 2
    return x * cosine + pltpu.roll(x, 128 - half, 1) * upper + pltpu.roll(x, half, 1) * lower


def keyvalue_kernel(tok, gain, bias, weight, kv_bias, cos, up, low, attn_in_ref, kv_ref, normed_ref, inverse_ref):
    normed, inverse = row_norm(tok[...].astype(F32))
    normed_ref[...] = normed
    inverse_ref[...] = jnp.broadcast_to(inverse, inverse_ref.shape)
    attn_in = (normed * gain[...] + bias[...]).astype(BF)
    attn_in_ref[...] = attn_in
    lin = dot(attn_in, weight[...]) + kv_bias[...]
    lane = lax.broadcasted_iota(jnp.int32, lin.shape, 1)
    turned = turn(lin, cos[...], up[...], low[...])
    kv_ref[...] = jnp.where(lane < 64, turned, lin).astype(BF)


def keyvalue_project(tokens, gain, bias, weight, kv_bias, planes, block):
    rows, width = tokens.shape
    local_len = planes[0].shape[0]
    per_seq = local_len // block
    row_spec = lambda cols: pl.BlockSpec((block, cols), lambda i: (i, 0))
    full = lambda shape: pl.BlockSpec(shape, lambda i: (0, 0))
    plane = pl.BlockSpec((block, 128), lambda i: (i % per_seq, 0))
    return pl.pallas_call(
        keyvalue_kernel,
        grid=(rows // block,),
        in_specs=[row_spec(width), full((1, width)), full((1, width)), full(weight.shape), full((1, 128))]
        + [plane] * 3,
        out_specs=[row_spec(width), row_spec(128), row_spec(width), row_spec(128)],
        out_shape=[
            jax.ShapeDtypeStruct((rows, width), BF),
            jax.ShapeDtypeStruct((rows, 128), BF),
            jax.ShapeDtypeStruct((rows, width), F32),
            jax.ShapeDtypeStruct((rows, 128), F32),
        ],
        compiler_params=pltpu.CompilerParams(vmem_limit_bytes=VMEM_LIMIT),
        cost_estimate=pl.CostEstimate(
            flops=2 * rows * width * 128, transcendentals=rows, bytes_accessed=rows * width * 4
        ),
        name="keyvalue_project",
    )(tokens, gain, bias, weight, kv_bias, *planes)


def query_kernel(block, per_seq, scalars, attn_in, cot, weight, q_bias, out_weight, cos, up, low, q_ref, mg_ref):
    step = pl.program_id(0)
    width = attn_in.shape[1]
    lin = dot(attn_in[...], weight[...]) + q_bias[...]
    scale = 64 ** (-0.5)
    for pair in range(width // 128):
        lanes = slice(pair * 128, (pair + 1) * 128)
        q_ref[:, lanes] = (turn(lin[:, lanes], cos[...], up[...], low[...]) * scale).astype(BF)
    start = scalars[0] + lax.rem(step, per_seq) * block
    position = start + lax.broadcasted_iota(jnp.int32, (block, 1), 0)
    live = position < scalars[1 + step // per_seq]
    grad = jnp.where(live, cot[...].astype(F32), 0.0).astype(BF)
    mg_ref[...] = dot_nt(grad, out_weight[...]).astype(BF)


def query_project(scalars, attn_in, cot, weight, q_bias, out_weight, planes, block):
    rows, width = attn_in.shape
    local_len = planes[0].shape[0]
    per_seq = local_len // block
    row_spec = pl.BlockSpec((block, width), lambda i, s: (i, 0))
    full = lambda shape: pl.BlockSpec(shape, lambda i, s: (0, 0))
    plane = pl.BlockSpec((block, 128), lambda i, s: (i % per_seq, 0))
    return pl.pallas_call(
        functools.partial(query_kernel, block, per_seq),
        grid_spec=pltpu.PrefetchScalarGridSpec(
            num_scalar_prefetch=1,
            grid=(rows // block,),
            in_specs=[row_spec, row_spec, full(weight.shape), full((1, width)), full(out_weight.shape)]
            + [plane] * 3,
            out_specs=[row_spec, row_spec],
        ),
        out_shape=[jax.ShapeDtypeStruct((rows, width), BF)] * 2,
        compiler_params=pltpu.CompilerParams(vmem_limit_bytes=VMEM_LIMIT),
        cost_estimate=pl.CostEstimate(
            flops=4 * rows * width * width, transcendentals=0, bytes_accessed=rows * width * 8 + width * width * 4
        ),
        name="query_project",
    )(scalars, attn_in, cot, weight, q_bias, out_weight, *planes)


def attention_kernel(chunk, pieces, scalars, q_ref, mg_ref, *refs):
    kv_refs, refs = refs[:pieces], refs[pieces:]
    (cos, up, low, o_ref, qg_ref), refs = refs[:5], refs[5:]
    dkv_refs, refs = refs[:pieces], refs[pieces:]
    key0, key1, val0, val1, key_t, val_t, sc, weights_sc, acc_k, acc_v, mix_t, qg_t, own = refs
    step = pl.program_id(0)
    offset, seq_len, index = scalars[0], scalars[1], scalars[2]
    rows = q_ref.shape[0]
    span = kv_refs[0].shape[0]
    keys, vals = (key0, key1), (val0, val1)
    left = lax.broadcasted_iota(jnp.int32, (1, 128), 1) < 64
    halves = (slice(0, 64), slice(64, 128))

    @pl.when(step == 0)
    def _():
        for distance in range(pieces):
            source = lax.rem(index + (pieces - distance), pieces)
            part = pl.ds(pl.multiple_of(source * span, span), span)
            kv = kv_refs[distance][...].astype(F32)
            key_left = jnp.where(left, kv, 0.0)
            val_right = jnp.where(left, 0.0, kv)
            key0[part, :] = key_left.astype(BF)
            key1[part, :] = pltpu.roll(key_left, 64, 1).astype(BF)
            val1[part, :] = val_right.astype(BF)
            val0[part, :] = pltpu.roll(val_right, 64, 1).astype(BF)
            kv_t = kv.T
            for start in range(0, span, chunk):
                place = source * (span // chunk) + start // chunk
                key_t[place] = kv_t[:64, start:start + chunk].astype(BF)
                val_t[place] = kv_t[64:, start:start + chunk].astype(BF)
            acc_k[part, :] = jnp.zeros((span, 128), F32)
            acc_v[part, :] = jnp.zeros((span, 128), F32)

    last = jnp.minimum(offset + rows, seq_len)
    count = (last + chunk - 1) // chunk
    whole = jnp.minimum(offset, seq_len) // chunk

    def score_step(masked, number, tops):
        part = pl.ds(pl.multiple_of(number * chunk, chunk), chunk)
        fresh = []
        for head in range(2):
            scores = dot_nt(keys[head][part, :], q_ref[...])
            if masked:
                col = number * chunk + lax.broadcasted_iota(jnp.int32, scores.shape, 0)
                row = offset + lax.broadcasted_iota(jnp.int32, scores.shape, 1)
                scores = jnp.where((col <= row) & (col < seq_len), scores, NEG_FILL)
            sc[head, number] = scores
            fresh.append(jnp.maximum(tops[head], jnp.max(scores, axis=0, keepdims=True)))
        return tuple(fresh)

    low_top = jnp.full((1, rows), NEG_FILL, F32)
    tops = lax.fori_loop(0, whole, functools.partial(score_step, False), (low_top, low_top))
    tops = lax.fori_loop(whole, count, functools.partial(score_step, True), tops)
    mix_t[...] = jnp.zeros(mix_t.shape, F32)

    def mix_step(number, sums):
        fresh = []
        for head in range(2):
            weights = jnp.exp(sc[head, number] - tops[head])
            fresh.append(sums[head] + jnp.sum(weights, axis=0, keepdims=True))
            low_weights = weights.astype(BF)
            weights_sc[head, number] = low_weights
            mix_t[halves[head], :] += dot(val_t[number], low_weights)
        return tuple(fresh)

    zero_row = jnp.zeros((1, rows), F32)
    sums = lax.fori_loop(0, count, mix_step, (zero_row, zero_row))
    inverses = [1.0 / s for s in sums]
    for head in range(2):
        mix_t[halves[head], :] *= inverses[head]
    mix = mix_t[...]
    o_ref[...] = mix.T.astype(BF)

    @pl.when(offset >= seq_len)
    def _():
        qg_ref[...] = jnp.zeros(qg_ref.shape, BF)

    @pl.when(offset < seq_len)
    def _():
        mix_grad = mg_ref[...].astype(F32)
        query = q_ref[...].astype(F32)
        products = mix * mix_grad.T
        dots = [jnp.sum(products[half, :], axis=0, keepdims=True) for half in halves]
        spread = jnp.concatenate([jnp.broadcast_to(i, (64, rows)) for i in inverses]).T
        query_f = query * spread
        mix_grad_f = mix_grad * spread
        own[0] = jnp.where(left, query_f, 0.0).astype(BF)
        own[1] = jnp.where(left, 0.0, query_f).astype(BF)
        own[2] = jnp.where(left, mix_grad_f, 0.0).astype(BF)
        own[3] = jnp.where(left, 0.0, mix_grad_f).astype(BF)
        qg_t[...] = jnp.zeros(qg_t.shape, F32)

        def grad_step(number, _):
            part = pl.ds(pl.multiple_of(number * chunk, chunk), chunk)
            new_k, new_v = acc_k[part, :], acc_v[part, :]
            for head in range(2):
                prob_grad = dot_nt(vals[head][part, :], mg_ref[...])
                low_weights = weights_sc[head, number]
                score_grad = (low_weights.astype(F32) * (prob_grad - dots[head])).astype(BF)
                qg_t[halves[head], :] += dot(key_t[number], score_grad)
                new_k = new_k + dot(score_grad, own[head])
                new_v = new_v + dot(low_weights, own[2 + head])
            acc_k[part, :] = new_k
            acc_v[part, :] = new_v
            return 0

        lax.fori_loop(0, count, grad_step, 0)
        query_grad = qg_t[...].T * (spread * 64 ** (-0.5))
        qg_ref[...] = turn(query_grad, cos[...], -up[...], -low[...]).astype(BF)

    @pl.when(step == pl.num_programs(0) - 1)
    def _():
        for distance in range(pieces):
            owner = lax.rem(index + distance, pieces)
            part = pl.ds(pl.multiple_of(owner * span, span), span)
            key_sum = acc_k[part, :]
            val_sum = acc_v[part, :]
            key_sum = key_sum + pltpu.roll(key_sum, 64, 1)
            val_sum = val_sum + pltpu.roll(val_sum, 64, 1)
            dkv_refs[distance][...] = jnp.where(left, key_sum, val_sum).astype(dkv_refs[distance].dtype)


def attention(scalars, q, mg, seq, kv, planes, chunk, earlier=()):
    all_rows, width = q.shape
    pieces = len(kv)
    rows = span = planes[0].shape[0]
    total = span * pieces
    pair = pl.BlockSpec((rows, 128), lambda i, s: (seq, i))
    plane = pl.BlockSpec((rows, 128), lambda i, s: (0, 0))
    own = pl.BlockSpec((span, 128), lambda i, s: (seq, 0))
    heads = width // 64
    inputs = [scalars, q, mg, *kv, *planes, *earlier]
    first = len(inputs) - len(earlier)

    def kernel(*refs):
        attention_kernel(chunk, pieces, *refs[:first], *refs[len(inputs) :])

    return pl.pallas_call(
        kernel,
        grid_spec=pltpu.PrefetchScalarGridSpec(
            num_scalar_prefetch=1,
            grid=(width // 128,),
            in_specs=[pair, pair]
            + [plane] * (pieces + 3)
            + [pl.BlockSpec(memory_space=pl.ANY)] * len(earlier),
            out_specs=[pair, pair] + [own] * pieces,
            scratch_shapes=[pltpu.VMEM((total, 128), BF)] * 4
            + [pltpu.VMEM((total // chunk, 64, chunk), BF)] * 2
            + [pltpu.VMEM((2, total // chunk, chunk, rows), F32)]
            + [pltpu.VMEM((2, total // chunk, chunk, rows), BF)]
            + [pltpu.VMEM((total, 128), F32)] * 2
            + [pltpu.VMEM((128, rows), F32)] * 2
            + [pltpu.VMEM((4, rows, 128), BF)],
        ),
        out_shape=[jax.ShapeDtypeStruct((all_rows, width), BF)] * 2
        + [jax.ShapeDtypeStruct((all_rows, 128), F32)]
        + [jax.ShapeDtypeStruct((all_rows, 128), BF)] * (pieces - 1),
        input_output_aliases={first + i: i for i in range(len(earlier))},
        compiler_params=pltpu.CompilerParams(vmem_limit_bytes=VMEM_LIMIT),
        cost_estimate=pl.CostEstimate(
            flops=12 * rows * heads * total * 256, transcendentals=rows * heads * total,
            bytes_accessed=rows * width * 8,
        ),
        name="attention",
    )(*inputs)


def feed_kernel(
    block, local_len, fold, scalars, normed, cot, side, inner, outer_rows, inner_bias,
    y_ref, dff_ref, grads_ref, dbias_ref, ff_in, grad, act, slope, outer,
):
    step = pl.program_id(0)
    rows, width = normed.shape
    units = inner.shape[1]
    part = units // fold
    spans = [pl.ds(start, block) for start in range(0, rows, block)]

    @pl.when(step == 0)
    def _():
        for number, span in enumerate(spans):
            ff_in[span, :] = (normed[span, :] * side[2:3, :] + side[3:4, :]).astype(BF)
            start = number * block
            position = scalars[0] + start % local_len + lax.broadcasted_iota(jnp.int32, (block, 1), 0)
            live = position < scalars[1 + start // local_len]
            grad[span, :] = jnp.where(live, cot[span, :].astype(F32), 0.0).astype(BF)
            y_ref[span, :] = jnp.zeros((block, width), F32)
            dff_ref[span, :] = jnp.zeros((block, width), F32)

    for j in range(fold):
        outer[j * part : (j + 1) * part, :] = outer_rows[:, j * width : (j + 1) * width]
    bias_sum = jnp.zeros((1, units), F32)
    for span in spans:
        pre = dot(ff_in[span, :], inner[...]) + inner_bias[...]
        back = dot_nt(grad[span, :], outer[...])
        share, density = gelu_parts(pre)
        act_part = (pre * share).astype(BF)
        slope_part = (back * (share + density)).astype(BF)
        act[span, :] = act_part
        slope[span, :] = slope_part
        bias_sum = bias_sum + jnp.sum(slope_part.astype(F32), axis=0, keepdims=True)
        y_ref[span, :] += dot(act_part, outer[...])
        dff_ref[span, :] += dot_nt(slope_part, inner[...])
    dbias_ref[...] = bias_sum
    columns = pl.ds(pl.multiple_of(step * units, units), units)
    grads_ref[:, columns] = dot_tn(ff_in[...], slope[...]).astype(BF)
    douter = dot_tn(act[...], grad[...]).astype(BF)
    lines = pl.ds(pl.multiple_of(step * part, part), part)
    hidden = fold * width
    for j in range(fold):
        grads_ref[lines, hidden + j * width : hidden + (j + 1) * width] = douter[j * part : (j + 1) * part, :]


def feed_forward(scalars, normed, cot, side, weights, inner_bias, local_len, block, units):
    rows, width = normed.shape
    hidden = weights.shape[1] // 2
    fold = hidden // width
    one = pl.Buffered(1)
    full = lambda shape: pl.BlockSpec(shape, lambda i, s: (0, 0), pipeline_mode=one)
    return pl.pallas_call(
        functools.partial(feed_kernel, block, local_len, fold),
        grid_spec=pltpu.PrefetchScalarGridSpec(
            num_scalar_prefetch=1,
            grid=(hidden // units,),
            in_specs=[
                full((rows, width)),
                full((rows, width)),
                full(side.shape),
                pl.BlockSpec((width, units), lambda i, s: (0, i)),
                pl.BlockSpec((units // fold, hidden), lambda i, s: (i, 1)),
                pl.BlockSpec((1, units), lambda i, s: (0, i)),
            ],
            out_specs=[
                full((rows, width)),
                full((rows, width)),
                full((width, 2 * hidden)),
                pl.BlockSpec((1, units), lambda i, s: (0, i)),
            ],
            scratch_shapes=[pltpu.VMEM((rows, width), BF)] * 2
            + [pltpu.VMEM((rows, units), BF)] * 2
            + [pltpu.VMEM((units, width), BF)],
        ),
        out_shape=[
            jax.ShapeDtypeStruct((rows, width), F32),
            jax.ShapeDtypeStruct((rows, width), F32),
            jax.ShapeDtypeStruct((width, 2 * hidden), BF),
            jax.ShapeDtypeStruct((1, hidden), F32),
        ],
        compiler_params=pltpu.CompilerParams(vmem_limit_bytes=VMEM_LIMIT),
        cost_estimate=pl.CostEstimate(
            flops=12 * rows * width * hidden, transcendentals=rows * hidden,
            bytes_accessed=rows * width * 12 + width * hidden * 8,
        ),
        name="feed_forward",
    )(scalars, normed, cot, side, weights, weights, inner_bias)


def live_grad(scalars, cot, seq, start):
    position = scalars[0] + start + lax.broadcasted_iota(jnp.int32, (cot.shape[0], 1), 0)
    return jnp.where(position < scalars[1 + seq], cot[...].astype(F32), 0.0)


def norm_sum_kernel(per_seq, pieces, shard, ways, scalars, normed, cot, attn_in, qlg, back, dff, *refs):
    kvs, refs = refs[:pieces], refs[pieces:]
    kv_weight, cos, up, low, bias_rows, query_grad, out_grad, attn_back_ref, *outs, packed_ref, kv_grad, sums = refs
    step = pl.program_id(0)
    width = normed.shape[1]

    @pl.when(step == 0)
    def _():
        kv_grad[...] = jnp.zeros(kv_grad.shape, F32)
        sums[...] = jnp.zeros(sums.shape, F32)

    kv = kvs[0][...]
    for piece in kvs[1:]:
        kv = kv + piece[...].astype(F32)
    kv = kv.astype(BF).astype(F32)
    lane = lax.broadcasted_iota(jnp.int32, kv.shape, 1)
    kv_lin = jnp.where(lane < 64, turn(kv, cos[...], -up[...], -low[...]), kv).astype(BF)
    attn_back = back[...] + dot_nt(kv_lin, kv_weight[...])
    attn_back_ref[...] = attn_back
    kv_grad[...] += dot_tn(attn_in[...], kv_lin)
    column = lambda x: jnp.sum(x, axis=0, keepdims=True)
    feed = dff[...]
    grad_out = live_grad(scalars, cot, step // per_seq, lax.rem(step, per_seq) * cot.shape[0])
    kv_bias = jnp.concatenate([column(kv_lin.astype(F32)), jnp.zeros((1, width - 128), F32)], axis=1)
    sums[...] += jnp.concatenate(
        [
            column(attn_back * normed[...]), column(attn_back), column(feed * normed[...]), column(feed),
            column(qlg[...].astype(F32)), column(grad_out), kv_bias, jnp.zeros((1, width), F32),
        ]
    )

    @pl.when(step == pl.num_programs(0) - 1)
    def _():
        values = jnp.concatenate([sums[0:6, :], jnp.zeros((2, width), F32), bias_rows[...]])
        values = jnp.concatenate([values, jnp.zeros((128 - values.shape[0], width), F32)]).T
        bias = jnp.broadcast_to(sums[6:7, :128], (8, 128))
        line = lax.rem(lax.broadcasted_iota(jnp.int32, (width, 128), 0), shard)
        spot = lax.broadcasted_iota(jnp.int32, (width, 128), 1)
        for third in range(3):
            moved = pltpu.roll(bias, (16 - 48 * third) % 128, 1)[0:1, :]
            values = values + jnp.where((line == third) & (spot >= 16) & (spot < 64), moved, 0.0)
        high = values.astype(BF).astype(F32)
        packed_ref[:, :128] = kv_grad[...]
        packed_ref[:, 128:] = high + pltpu.roll(values - high, 64, 1)
        if not ways:
            outs[0][:, :width] = query_grad[...]
            outs[0][:, width : 2 * width] = out_grad[...]
            outs[0][:, 2 * width :] = packed_ref[...].astype(BF)
        for slot, way in enumerate(ways):
            for mask, target in enumerate(outs):
                lines = target.shape[1]
                block = scalars[scalars.shape[0] - 1] ^ way ^ mask
                part = pl.ds(pl.multiple_of(block * lines, lines), lines)
                target[slot, :, :width] = query_grad[part, :]
                target[slot, :, width : 2 * width] = out_grad[part, :]
                target[slot, :, 2 * width :] = packed_ref[part, :].astype(BF)


def norm_sums(scalars, normed, cot, attn_in, qlg, back, dff, kvs, kv_weight, planes, bias_rows, wide, shard, block, ways):
    rows, width = normed.shape
    per_seq = planes[0].shape[0] // block
    own = lambda cols: pl.BlockSpec((block, cols), lambda i, s: (i, 0))
    full = lambda shape: pl.BlockSpec(shape, lambda i, s: (0,) * len(shape))
    plane = pl.BlockSpec((block, 128), lambda i, s: (i % per_seq, 0))
    columns = 2 * width + 256
    shapes = [(len(ways), width // (2 * len(ways)), columns)] * 2 if ways else [(width, columns)]
    return pl.pallas_call(
        functools.partial(norm_sum_kernel, per_seq, len(kvs), shard, ways),
        grid_spec=pltpu.PrefetchScalarGridSpec(
            num_scalar_prefetch=1,
            grid=(rows // block,),
            in_specs=[own(width)] * 6
            + [own(128)] * len(kvs)
            + [full(kv_weight.shape)]
            + [plane] * 3
            + [full((8, width))]
            + [full((width, width))] * 2,
            out_specs=[own(width)] + [full(shape) for shape in shapes],
            scratch_shapes=[
                pltpu.VMEM((width, 256), F32), pltpu.VMEM((width, 128), F32), pltpu.VMEM((8, width), F32),
            ],
        ),
        out_shape=[jax.ShapeDtypeStruct((rows, width), F32)] + [jax.ShapeDtypeStruct(shape, BF) for shape in shapes],
        compiler_params=pltpu.CompilerParams(vmem_limit_bytes=VMEM_LIMIT),
        cost_estimate=pl.CostEstimate(
            flops=4 * rows * width * 128, transcendentals=0, bytes_accessed=rows * width * 20
        ),
        name="norm_sums",
    )(scalars, normed, cot, attn_in, qlg, back, dff, *kvs, kv_weight, *planes, bias_rows, *wide)


def token_grad_kernel(per_seq, scalars, normed_ref, cot, attn_back, dff, inverse, side, token_grads_ref):
    step = pl.program_id(0)
    block = cot.shape[0]
    grad_out = live_grad(scalars, cot, step // per_seq, lax.rem(step, per_seq) * block)
    normed = normed_ref[...]
    normed_grad = attn_back[...] * side[0:1, :] + dff[...] * side[2:3, :]
    mean = jnp.mean(normed_grad, axis=-1, keepdims=True)
    match = jnp.mean(normed_grad * normed, axis=-1, keepdims=True)
    token_grads_ref[...] = grad_out + inverse[:, 0:1] * (normed_grad - mean - normed * match)


def token_grad(scalars, normed, cot, attn_back, dff, inverse, side, local_len, block):
    rows, width = normed.shape
    own = pl.BlockSpec((block, width), lambda i, s: (i, 0))
    return pl.pallas_call(
        functools.partial(token_grad_kernel, local_len // block),
        grid_spec=pltpu.PrefetchScalarGridSpec(
            num_scalar_prefetch=1,
            grid=(rows // block,),
            in_specs=[own] * 4
            + [pl.BlockSpec((block, 128), lambda i, s: (i, 0)), pl.BlockSpec(side.shape, lambda i, s: (0, 0))],
            out_specs=own,
        ),
        out_shape=jax.ShapeDtypeStruct((rows, width), F32),
        compiler_params=pltpu.CompilerParams(vmem_limit_bytes=VMEM_LIMIT),
        cost_estimate=pl.CostEstimate(flops=20 * rows * width, transcendentals=0, bytes_accessed=rows * width * 16),
        name="token_grad",
    )(scalars, normed, cot, attn_back, dff, inverse, side)


def shift_perm(distance, count):
    return [(i, (i + distance) % count) for i in range(count)]


def flip_perm(mask, count):
    return [(i, i ^ mask) for i in range(count)]


def dp_groups():
    bits = [1 << b for b in range((lax.axis_size("dp") - 1).bit_length())]
    rest = bits[1:]
    return [bits[:1]] + [rest[i : i + 2] for i in range(0, len(rest), 2)]


def combinations(bits):
    masks = [0]
    for bit in bits:
        masks += [m | bit for m in masks]
    return masks


def place_kernel(ways, count, key_counts, cuts, scalars, *refs):
    ins, outs = refs[: len(key_counts)], refs[len(key_counts) :]
    key = 0
    for ref, keys in zip(ins, key_counts):
        for slot in range(keys):
            for distance in range(count):
                source = lax.rem(scalars[1] + (count - distance), count)
                place = (scalars[0] ^ ways[key]) * count + source
                for out, start, end in zip(outs, cuts, cuts[1:]):
                    out[place] = ref[slot, distance, :, start:end].astype(out.dtype)
            key += 1
    if len(outs) > len(cuts) - 1:
        outs[-1][...] = outs[-2][...].reshape(-1, 128).T[:16, :]


def gather_all(x, cuts, dp_index, context_index, riders):
    size, count = lax.axis_size("dp"), lax.axis_size("ctx")
    column = jnp.stack([x] + [lax.ppermute(x, "ctx", shift_perm(d, count)) for d in range(1, count)])
    column, *riders = lax.optimization_barrier((column, *riders))
    stacks, ways = [column[None]], [0]
    for bits in reversed(dp_groups()):
        own = stacks[0] if len(stacks) == 1 else jnp.concatenate(stacks)
        arrived, new_ways = [], []
        for mask in combinations(bits)[1:]:
            arrived.append(lax.ppermute(own, "dp", flip_perm(mask, size)))
            new_ways += [w ^ mask for w in ways]
        stacks, ways = [own] + arrived, ways + new_ways
    blocks = [(size * count, x.shape[0], e - b) for b, e in zip(cuts, cuts[1:])]
    shapes = [jax.ShapeDtypeStruct(block, x.dtype) for block in blocks[:-1]] + [jax.ShapeDtypeStruct(blocks[-1], F32)]
    aligned = x.shape[0] % 8 == 0
    if aligned:
        shapes.append(jax.ShapeDtypeStruct((16, blocks[-1][0] * blocks[-1][1]), F32))
    *gathered, side = pl.pallas_call(
        functools.partial(place_kernel, ways, count, [s.shape[0] for s in stacks], cuts),
        grid_spec=pltpu.PrefetchScalarGridSpec(
            num_scalar_prefetch=1,
            grid=(1,),
            in_specs=[pl.BlockSpec(s.shape, lambda i, s: (0, 0, 0, 0)) for s in stacks],
            out_specs=[pl.BlockSpec(s.shape, lambda i, _, n=len(s.shape): (0,) * n) for s in shapes],
        ),
        out_shape=shapes,
        compiler_params=pltpu.CompilerParams(vmem_limit_bytes=VMEM_LIMIT),
        name="place",
    )(jnp.stack([dp_index, context_index]), *stacks)
    if not aligned:
        side = side.reshape(-1, 128)[:, :16].T
    return gathered[: len(cuts) - 2] + [side], riders


def pack_kernel(fold, *refs):
    *vectors, inner_bias, query, output, keyvalue, out = refs
    shard, width = query.shape
    rows = [v[...].astype(F32) for v in vectors] + [
        inner_bias[:, j * shard : (j + 1) * shard].astype(F32) for j in range(fold)
    ]
    lines = jnp.concatenate(rows + [jnp.zeros((128 - len(rows), shard), F32)])
    out[:, :width] = query[...]
    out[:, width : 2 * width] = output[...]
    out[:, 2 * width : 2 * width + 128] = keyvalue[...]
    out[:, 2 * width + 128 :] = lines.T.astype(BF)


def pack(vectors, inner_bias, query, output, keyvalue, fold):
    args = [v[None] for v in vectors] + [inner_bias[None], query, output, keyvalue]
    shape = (query.shape[0], 2 * query.shape[1] + 256)
    return pl.pallas_call(
        functools.partial(pack_kernel, fold),
        grid=(1,),
        in_specs=[pl.BlockSpec(x.shape, lambda i: (0, 0)) for x in args],
        out_specs=pl.BlockSpec(shape, lambda i: (0, 0)),
        out_shape=jax.ShapeDtypeStruct(shape, BF),
        name="pack",
    )(*args)


def core_keys():
    return list(range(0, lax.axis_size("dp"), 2))


def settle(x):
    value = x[..., -128:-64] + x[..., -64:]
    high = lax.reduce_precision(value, 8, 7)
    return jnp.concatenate([x[..., :-128].astype(BF), high.astype(BF), (value - high).astype(BF)], axis=-1)


def add_pairs(parts):
    while len(parts) > 1:
        parts = [a + b for a, b in zip(parts[::2], parts[1::2])]
    return parts[0]


def scatter_blocks(keep, send, context_index, fillers):
    size, count = lax.axis_size("dp"), lax.axis_size("ctx")
    fillers = list(fillers)
    filled = []

    def beside(parts):
        if fillers:
            *parts, extra = lax.optimization_barrier((*parts, fillers.pop(0)()))
            filled.append(extra)
        return [p.astype(F32) for p in parts]

    arrived = lax.ppermute(send, "dp", flip_perm(1, size))
    total = settle(add_pairs(beside([keep, arrived])))
    held = {key: total[slot] for slot, key in enumerate(core_keys())}
    for bits in dp_groups()[1:]:
        keys = [k for k in held if not any(k & bit for bit in bits)]
        parts = [jnp.stack([held[k] for k in keys])]
        for mask in combinations(bits)[1:]:
            parts.append(lax.ppermute(jnp.stack([held[k ^ mask] for k in keys]), "dp", flip_perm(mask, size)))
        total = settle(add_pairs(beside(parts)))
        held = {key: total[slot] for slot, key in enumerate(keys)}
    column = held[0].reshape(count, -1, keep.shape[-1])
    pick = lambda mask: lax.dynamic_index_in_dim(column, context_index ^ mask, 0, keepdims=False)
    parts = [pick(0)]
    bits = [1 << b for b in range((count - 1).bit_length())]
    for mask in combinations(bits)[1:]:
        parts.append(lax.ppermute(pick(mask), "ctx", flip_perm(mask, count)))
    while fillers:
        *parts, extra = lax.optimization_barrier((*parts, fillers.pop(0)()))
        filled.append(extra)
    return parts, filled


def split_blocks(x, dp_index):
    x = x.reshape(lax.axis_size("dp"), -1, x.shape[-1])
    pick = lambda key: lax.dynamic_index_in_dim(x, dp_index ^ key, 0, keepdims=False)
    return jnp.stack([pick(key) for key in core_keys()]), jnp.stack([pick(key ^ 1) for key in core_keys()])


def finish_kernel(count, fold, *refs):
    parts, refs = refs[:count], refs[count:]
    query_ref, output_ref, kv_ref, inner_bias_ref, kv_bias_ref = refs[:5]
    total = add_pairs([part[...].astype(F32) for part in parts])
    width = query_ref.shape[1]
    query_ref[...] = total[:, :width]
    output_ref[...] = total[:, width : 2 * width]
    kv_ref[...] = total[:, 2 * width : 2 * width + 128]
    values = total[:, 2 * width + 128 :]
    values = values + pltpu.roll(values, 64, 1)
    spot = lax.broadcasted_iota(jnp.int32, (1, 128), 1)
    bias = jnp.zeros((1, 128), F32)
    for third in range(3):
        moved = pltpu.roll(jnp.broadcast_to(values[third : third + 1, :], (8, 128)), (48 * third - 16) % 128, 1)[0:1, :]
        bias = jnp.where((spot >= 48 * third) & (spot < 48 * third + 48), moved, bias)
    kv_bias_ref[...] = bias
    shard = values.shape[0]
    lines = jnp.concatenate([values, jnp.zeros((128 - shard, 128), F32)]).T
    spot = lax.broadcasted_iota(jnp.int32, (1, 128), 1)
    bias = jnp.zeros((1, 128), F32)
    for j in range(fold):
        moved = pltpu.roll(jnp.broadcast_to(lines[8 + j : 9 + j, :], (8, 128)), j * shard, 1)[0:1, :]
        bias = jnp.where((spot >= j * shard) & (spot < (j + 1) * shard), moved, bias)
    inner_bias_ref[...] = bias[:, : fold * shard]
    for number, ref in zip((0, 1, 2, 3, 4, 5, 5), refs[5:]):
        ref[...] = lines[number : number + 1, :shard]


def finish(parts, width, fold):
    shard = parts[0].shape[0]
    shapes = [(shard, width), (shard, width), (shard, 128), (1, fold * shard), (1, 128)] + [(1, shard)] * 7
    full = lambda shape: pl.BlockSpec(shape, lambda i: (0, 0))
    return pl.pallas_call(
        functools.partial(finish_kernel, len(parts), fold),
        grid=(1,),
        in_specs=[full(p.shape) for p in parts],
        out_specs=[full(shape) for shape in shapes],
        out_shape=[jax.ShapeDtypeStruct(shape, F32) for shape in shapes],
        name="finish",
    )(*parts)


def local(
    tokens,
    seq_lengths,
    attention_gain,
    attention_bias,
    query_weight,
    query_bias,
    keyvalue_weight,
    keyvalue_bias,
    output_weight,
    output_bias,
    feedforward_gain,
    feedforward_bias,
    inner_weight,
    inner_bias,
    outer_weight,
    outer_bias,
    cotangent,
):
    seqs, local_len, width = tokens.shape
    head_size = keyvalue_weight.shape[1] // 2
    rows = seqs * local_len
    shard = query_weight.shape[0]
    hidden = inner_weight.shape[1]
    context_index = lax.axis_index("ctx")
    count = lax.axis_size("ctx")
    device_index = lax.axis_index("dp") * count + context_index
    block = min(256, local_len)
    chunk = min(512, local_len)
    offset = context_index * local_len
    position = offset + jnp.arange(local_len, dtype=jnp.int32)
    planes = rotary_planes(position, head_size)
    scalars = jnp.concatenate([offset[None].astype(jnp.int32), seq_lengths])
    wide = jnp.concatenate([scalars, lax.axis_index("dp")[None].astype(jnp.int32)])
    tok = tokens.reshape(rows, width)
    cot = cotangent.reshape(rows, width)

    dp_index = lax.axis_index("dp")
    devices = lax.axis_size("dp") * count
    vectors = [attention_gain, attention_bias, feedforward_gain, feedforward_bias, query_bias, output_bias, outer_bias]
    fold = hidden // width
    packed = pack(vectors, inner_bias, query_weight, output_weight, keyvalue_weight, fold)
    cuts = (0, width, 2 * width, 2 * width + 128, 2 * width + 256)
    (*gathered, side), raw = gather_all(packed, cuts, dp_index, context_index, (inner_weight, outer_weight))
    query_full, output_full, keyvalue_full = [g.reshape(width, -1) for g in gathered]
    gain_attn, bias_attn, q_shift = [side[i : i + 1] for i in (0, 1, 4)]

    units = min(768, hidden)
    owners = units // (fold * shard)

    def unit_order_bf16(x, back=False):
        here = jnp.arange(units)
        there = (here // shard % owners) * (fold * shard) + here // (owners * shard) * shard + here % shard
        turned = (here[:, None] == there[None, :]).astype(BF)
        turned = turned.T if back else turned
        parts = [dot(x[:, i : i + units], turned) for i in range(0, hidden, units)]
        return jnp.concatenate(parts, axis=1)

    inner_shift = side[7 : 7 + fold].reshape(fold, hidden // units, -1).swapaxes(0, 1).reshape(1, hidden)
    late = raw[1].reshape(fold, shard, width).swapaxes(0, 1).reshape(shard, hidden)
    late = jnp.concatenate([unit_order_bf16(raw[0]).astype(BF), late], axis=1)
    late = lax.all_gather(late, AXES, axis=0, tiled=True)
    kv_shift = keyvalue_bias.astype(F32)[None, :]

    attn_in, kv_own, normed, inverse = keyvalue_project(tok, gain_attn, bias_attn, keyvalue_full, kv_shift, planes, block)
    q, mg = query_project(scalars, attn_in, cot, query_full, q_shift, output_full, planes, block)

    ring = lambda x, d: lax.ppermute(x, "ctx", shift_perm(d, count))

    def rings(first, rest):
        return [first] + [ring(x, d) for d, x in enumerate(rest, 1)]

    kv_pieces = [kv_own[s * local_len : (s + 1) * local_len] for s in range(seqs)]
    kv_all = [rings(kv_pieces[0], [kv_pieces[0]] * (count - 1))]
    *kv_all[0], q, mg = lax.optimization_barrier((*kv_all[0], q, mg))
    *kv_pieces, q = lax.optimization_barrier((*kv_pieces, q))
    kv_all += [rings(piece, [piece] * (count - 1)) for piece in kv_pieces[1:]]
    places = [jnp.stack([scalars[0], scalars[1 + s], context_index]) for s in range(seqs)]
    results = attention(places[0], q, mg, 0, kv_all[0], planes, chunk)
    scalars_ff, results, kv_all[1:] = lax.optimization_barrier((scalars, results, kv_all[1:]))
    y_ff, ff_in_grad, late_grads, inner_grad_b = feed_forward(
        scalars_ff, normed, cot, side, late, inner_shift, local_len, block, units
    )
    bias_rows = inner_grad_b.reshape(hidden // units, fold, -1).swapaxes(0, 1).reshape(fold, width)
    bias_rows = jnp.pad(bias_rows, ((0, 8 - fold), (0, 0)))
    late_shard = lax.psum_scatter(late_grads, "dp", scatter_dimension=0, tiled=True)
    y_ff, places = lax.optimization_barrier((y_ff, places))
    for s in range(1, seqs):
        results = attention(places[s], q, mg, s, kv_all[s], planes, chunk, results)
    out, qlg, *kv_grads = results
    kv_sums = rings(kv_grads[0], kv_grads[1:])

    live = (position[None, :] < seq_lengths[:, None]).reshape(rows, 1)
    grad_out = jnp.where(live, cot, jnp.zeros((), BF))
    back = dot_nt(qlg, query_full)
    query_grad_w = dot_tn(attn_in, qlg).astype(BF)
    output_grad_w = dot_tn(out, grad_out).astype(BF)
    aligned = (shard * count) % 16 == 0
    attn_back, *blocks = norm_sums(
        wide, normed, cot, attn_in, qlg, back, ff_in_grad, kv_sums, keyvalue_full, planes, bias_rows,
        (query_grad_w, output_grad_w), shard, block, core_keys() if aligned else [],
    )
    keep, send = blocks if aligned else split_blocks(blocks[0], dp_index)
    late_shard, send = lax.optimization_barrier((late_shard, send))
    late_shard = lax.psum_scatter(late_shard, "ctx", scatter_dimension=0, tiled=True)
    attn_back, out, send = lax.optimization_barrier((attn_back, out, send))

    def last_outputs():
        branch = dot(out, output_full) + side[5:6]
        return (tok.astype(F32) + branch + (y_ff + side[6:7])).astype(BF)

    def last_token_grads():
        return token_grad(scalars, normed, cot, attn_back, ff_in_grad, inverse, side, local_len, block)

    parts, (outputs, token_grads) = scatter_blocks(keep, send, context_index, [last_outputs, last_token_grads])
    inner_shard = unit_order_bf16(late_shard[:, :hidden], True)
    outer_shard = late_shard[:, hidden:].astype(F32).reshape(shard, fold, width).swapaxes(0, 1).reshape(-1, width)
    query_shard, output_shard, kv_shard, bi, kvb, *lines = finish(parts, width, fold)
    ag, ab, fg, fb, bq, bo, b_outer = [line[0] for line in lines]
    return (
        outputs.reshape(tokens.shape),
        token_grads.reshape(tokens.shape),
        ag,
        ab,
        query_shard,
        bq,
        kv_shard,
        kvb[0],
        output_shard,
        bo,
        fg,
        fb,
        inner_shard,
        bi[0],
        outer_shard,
        b_outer,
    )


def solution(mesh):
    shard = P(("dp", "ctx"))
    matrix = P(("dp", "ctx"), None)
    token = P("dp", "ctx", None)
    in_specs = (
        token, P("dp"), shard, shard, matrix, shard, matrix, P(), matrix, shard,
        shard, shard, matrix, shard, matrix, shard, token,
    )
    out_specs = (
        token, token, shard, shard, matrix, shard, matrix, P(), matrix, shard,
        shard, shard, matrix, shard, matrix, shard,
    )
    return jax.shard_map(local, mesh=mesh, in_specs=in_specs, out_specs=out_specs, check_vma=False)
```
